32 devices in a mesh: readout: 8 (over y, x, core), frame: 4 (over z).
Axes of the slice: x: 2, y: 2, z: 4, core: 2. Of those that a mesh axis runs over, the one named last changes fastest.
Arguments:
- equilibrium: float32 [2, 8, 16, 128, 128], P(None, 'frame', 'readout'), may hold values from -6 to 6
- cotangent: float32 [2, 8, 16, 128, 128], P(None, 'frame', 'readout'), may hold values from -8 to 8
- sensitivity: float32 [2, 8, 16, 128, 128], P(None, None, 'readout'), may hold values from -1.5 to 1.5
- sampling: int32 [8, 8, 128, 128], P('frame'), may hold values 0 or 1
- weight_in: bfloat16 [24, 2, 3, 3, 3], replicated, may hold values from -0.875 to 0.875
- bias_in: float32 [24], replicated, may hold values from -4 to 4
- weight_mid: bfloat16 [24, 24, 3, 3, 3], replicated, may hold values from -0.25 to 0.25
- bias_mid: float32 [24], replicated, may hold values from -4 to 4
- weight_out: bfloat16 [2, 24, 3, 3, 3], replicated, may hold values from -0.25 to 0.25
Outputs:
- adjoint: float32 [2, 8, 16, 128, 128], P(None, 'frame', 'readout')
The draws below stay inside these ranges and needn't reach their ends.
Inputs may be any that keep to these rules, and one draw needn't show every extreme that they name: `sampling`: 1 where the k-space sample is acquired for that frame and coil, else 0.
All inputs are finite; a program needn't handle non-finite values. No bound on the sum of `sampling` on one device may be relied on, other than what follows from the above.
Results may differ from the reference program's by a relative error of at most 0.0024.
Values may be sent and summed in bfloat16 or wider, within the bound.
No kernel may reach another device: no remote copies, remote signals or barrier semaphores. Data moves between devices by JAX's collectives and lax.ppermute only.
A program may use at most 128 MiB of HBM per device.

```python
import jax
import jax.numpy as jnp
from jax import lax

NY = 128
NZ = 128
COILS = 8
CH = 24
ITERS = 2
DEPTH = 5
NT = 8
NX = 16


def draw_cotangent(key, part):
    spots = jnp.arange(NX, dtype=jnp.float32) / max(NX - 1, 1)
    ramp = 0.6 + 1.2 * spots
    field = jnp.clip(jax.random.normal(key, (2, NT, NX, NY, NZ), jnp.float32), -4.0, 4.0)
    return field * ramp[None, None, :, None, None]


def touch_ends(result, key, smallest, top_value):
    spot = [jax.random.randint(jax.random.fold_in(key, axis), (), 0, length) for axis, length in enumerate(result.shape)]
    widest = result.shape.index(max(result.shape))
    next_to = spot[:widest] + [(spot[widest] + 1) % result.shape[widest]] + spot[widest + 1:]
    return result.at[tuple(spot)].set(smallest).at[tuple(next_to)].set(top_value)


def level_of(own_key, extent, cuts, low, high):
    def one(axis_at, blocks):
        steps = jax.random.uniform(jax.random.fold_in(jax.random.fold_in(own_key, 6), axis_at), (blocks,), jnp.float32, low / len(cuts), high / len(cuts))
        return jnp.repeat(jnp.exp(steps), extent[axis_at] // blocks).reshape((-1,) + (1,) * (len(extent) - axis_at - 1))

    loudness = one(*cuts[0])
    for cut in cuts[1:]:
        loudness = loudness * one(*cut)
    return loudness


def bell_draw(own_key, dims, spread, reach, shards=(), kind=jnp.bfloat16):
    drawn = jax.random.normal(own_key, dims, jnp.float32) * spread
    if len(shards) > 0:
        drawn = level_of(own_key, dims, shards, -0.22, 0.18) * drawn
    return jnp.clip(drawn, min=-reach, max=reach).astype(kind)


def setup_inputs(seed: int = 0) -> dict:
    streams_of = jax.random.split(jax.random.key(seed), 10)
    equilibrium = bell_draw(streams_of[0], (2, NT, NX, NY, NZ), 1.0, 6.0, ((1, 4), (2, 8)), jnp.float32)
    cotangent = draw_cotangent(jax.random.fold_in(streams_of[9], 71), 0)
    sensitivity = bell_draw(streams_of[2], (2, COILS, NX, NY, NZ), 0.25, 1.5, ((2, 8),), jnp.float32)
    sampling = touch_ends((jax.random.randint(streams_of[3], (NT, COILS, NY, NZ), 0, 3) < 1).astype(jnp.int32), jax.random.fold_in(streams_of[3], 1), 0, 1)
    weight_in = bell_draw(streams_of[4], (CH, 2, 3, 3, 3), 54 ** -0.5, 0.875)
    bias_in = bell_draw(streams_of[5], (CH,), 1.0, 4.0, (), jnp.float32)
    weight_mid = bell_draw(streams_of[6], (CH, CH, 3, 3, 3), (27 * CH) ** -0.5, 0.25)
    bias_mid = bell_draw(streams_of[7], (CH,), 1.0, 4.0, (), jnp.float32)
    weight_out = bell_draw(streams_of[8], (2, CH, 3, 3, 3), (27 * CH) ** -0.5, 0.25)
    return {"equilibrium": equilibrium, "cotangent": cotangent, "sensitivity": sensitivity, "sampling": sampling, "weight_in": weight_in, "bias_in": bias_in, "weight_mid": weight_mid, "bias_mid": bias_mid, "weight_out": weight_out}


ETA = 0.5
RIDGE = 1e-4


def correlate(padded, kernel):
    return lax.conv_general_dilated(padded, kernel, (1, 1, 1), "VALID", dimension_numbers=("CTXYN", "OITXY", "CTXYN"), preferred_element_type=jnp.float32)


def pad_all(field):
    return jnp.pad(field, ((0, 0), (1, 1), (1, 1), (1, 1), (0, 0)))


def flip_kernel(weight):
    return jnp.transpose(jnp.flip(weight, (2, 3, 4)), (1, 0, 2, 3, 4))


def silu_slope(value):
    sigma = jax.nn.sigmoid(value)
    return sigma * (1.0 + value * (1.0 - sigma))


def small_solve(matrix, target):
    order = target.shape[0]
    lines = [matrix[index] for index in range(order)]
    values = [target[index] for index in range(order)]
    for column in range(order):
        for line in range(column + 1, order):
            factor = lines[line][column] / lines[column][column]
            lines[line] = lines[line] - factor * lines[column]
            values[line] = values[line] - factor * values[column]
    solution = [None] * order
    for line in reversed(range(order)):
        running = values[line]
        for column in range(line + 1, order):
            running = running - lines[line][column] * solution[column]
        solution[line] = running / lines[line][line]
    return jnp.stack(solution)


def reference(equilibrium, cotangent, sensitivity, sampling, weight_in, bias_in, weight_mid, bias_mid, weight_out):
    start_image = equilibrium.astype(jnp.bfloat16)
    pre_one = correlate(pad_all(start_image), weight_in) + bias_in[:, None, None, None, None]
    hidden = jax.nn.silu(pre_one).astype(jnp.bfloat16)
    slope_one = silu_slope(pre_one).astype(jnp.bfloat16)
    pre_two = correlate(pad_all(hidden), weight_mid) + bias_mid[:, None, None, None, None]
    slope_two = silu_slope(pre_two).astype(jnp.bfloat16)
    back_out = flip_kernel(weight_out)
    back_mid = flip_kernel(weight_mid)
    back_in = flip_kernel(weight_in)
    coil_maps = lax.complex(sensitivity[0], sensitivity[1])[:, None]
    mask_block = jnp.transpose(sampling, (1, 0, 2, 3))[:, :, None].astype(sensitivity.dtype)

    def transpose_net(field):
        rounded = field.astype(jnp.bfloat16)
        grad_two = (slope_two * correlate(pad_all(rounded), back_out)).astype(jnp.bfloat16)
        grad_one = (slope_one * correlate(pad_all(grad_two), back_mid)).astype(jnp.bfloat16)
        return correlate(pad_all(grad_one), back_in)

    def normal_op(field):
        values = lax.complex(field[0], field[1])[None]
        kspace = jnp.fft.fft2(coil_maps * values, axes=(3, 4), norm="ortho")
        images = jnp.fft.ifft2(kspace * mask_block, axes=(3, 4), norm="ortho")
        total = jnp.sum(jnp.conj(coil_maps) * images, axis=0)
        return jnp.stack([jnp.real(total), jnp.imag(total)])

    current = cotangent
    mapped_list = []
    residuals = []
    gram = {}
    for step in range(ITERS):
        mapped = cotangent + current - ETA * normal_op(current) - transpose_net(current)
        residual = mapped - current
        mapped_list.append(mapped)
        residuals.append(residual)
        first = max(0, step + 1 - DEPTH)
        window = list(range(first, step + 1))
        for older in window:
            gram[(step, older)] = jnp.sum(residual * residuals[older])
        count = len(window)
        if count == 1:
            current = mapped
        else:
            matrix = jnp.stack([jnp.stack([gram[(max(left, right), min(left, right))] for right in window]) for left in window])
            ridge = RIDGE * jnp.trace(matrix) / count
            matrix = matrix + ridge * jnp.eye(count, dtype=matrix.dtype)
            solution = small_solve(matrix, jnp.ones((count,), matrix.dtype))
            alpha = solution / jnp.sum(solution)
            current = alpha[0] * mapped_list[window[0]]
            for position in range(1, count):
                current = current + alpha[position] * mapped_list[window[position]]
    return current
```

```python
import functools
import math

import jax
import jax.numpy as jnp
import numpy as np
from jax import lax
from jax.experimental import pallas as pl
from jax.experimental.pallas import tpu as pltpu
from jax.sharding import PartitionSpec as P

ETA = 0.5
RIDGE = 0.0001
AXES = ("readout", "frame")
F32 = jnp.float32
BF16 = jnp.bfloat16
VMEM = pl.BlockSpec(memory_space=pltpu.VMEM)
GROUP = 8
WIDE = 16


class Plan:
    def __init__(self, devices_x, devices_t, frames, width, ny, nz, channels):
        self.R, self.F, self.tl, self.xl = devices_x, devices_t, frames, width
        self.ny, self.nz, self.ch = ny, nz, channels
        self.D = devices_x * devices_t
        self.T, self.X = frames * devices_t, width * devices_x
        self.zl = nz // self.D
        self.nzb = min(2, self.zl)
        self.NZB = self.zl // self.nzb
        self.L = self.nzb * ny
        self.unit = frames * 2 * width
        self.rows = self.X * channels
        self.M = GROUP * channels
        self.G = self.X // GROUP
        if self.G == 1:
            self.W, self.ws = self.M, [0]
        else:
            self.W = self.M + 32 if self.G == 2 else self.M + 64
            self.ws = [min(max(self.M * g - 32, 0), self.rows - self.W) for g in range(self.G)]
        self.GI = self.X // WIDE
        near = WIDE // width
        self.near = near
        extra = 0 if self.GI == 1 else 2
        self.UW = (near + extra) * self.unit
        self.us = [min(max(near * g - extra // 2, 0), devices_x - near - extra) for g in range(self.GI)]
        wide = WIDE * channels
        self.KW = wide if self.GI == 1 else wide + 64
        self.ks = [min(max(wide * g - 32, 0), self.rows - self.KW) for g in range(self.GI)]

    def mid_table(self, g):
        k = np.arange(9 * self.W)
        row = self.ws[g] + k % self.W
        tap = k // self.W
        return pack(tap * self.ch + row % self.ch, row // self.ch)

    def in_table(self, g, t2):
        k = np.arange(9 * self.UW)
        slot, c, rest = k // (3 * self.UW), k // self.UW % 3, k % self.UW
        r, rest = self.us[g] + rest // self.unit, rest % self.unit
        frame, part, x2 = rest // (2 * self.xl), rest // self.xl % 2, rest % self.xl
        a = self.tl * (slot - 1) + frame - t2 + 1
        q = np.where((a >= 0) & (a <= 2), (a * 3 + c) * 2 + part, -1)
        return pack(q, r * self.xl + x2)

    def out_rows(self, g, s):
        m = np.arange(2 * 3 * self.near * self.unit)
        target, rest = m // (3 * self.near * self.unit), m % (3 * self.near * self.unit)
        c, rest = rest // (self.near * self.unit), rest % (self.near * self.unit)
        r, rest = self.near * g + rest // self.unit, rest % self.unit
        frame, part, x2 = rest // (2 * self.xl), rest // self.xl % 2, rest % self.xl
        offset = self.tl if s == 0 else -self.tl
        a = s - frame + 1 + np.where(target == 1, offset, 0)
        q = np.where((a >= 0) & (a <= 2), (a * 3 + c) * 2 + part, -1)
        pick = (q[:, None] == np.arange(24)[None, :]).astype(np.float32).astype(BF16)
        return pick, (r * self.xl + x2).astype(np.int32)

    def out_cols(self, g):
        row = self.ks[g] + np.arange(self.KW)
        return pack(row % self.ch, row // self.ch)


def pack(q, position):
    return np.stack([q, position] + [np.zeros_like(q)] * 6).astype(np.int32)


def dot(a, b):
    return jnp.dot(a, b, preferred_element_type=F32)


def one_hot_rows(table, rows):
    k = table.shape[1]
    index = lax.broadcasted_iota(jnp.int32, (rows, k), 0)
    return (index == jnp.broadcast_to(table[0:1, :], (rows, k))).astype(F32).astype(BF16)


def banded(weights, table, first, count, channels, out_ref, where, row0):
    spread = dot(weights, one_hot_rows(table, weights.shape[1]))
    parts = [spread[b * channels : (b + 1) * channels] for b in range(3)]
    position = table[1:2, :]
    for pair in range(count // 2):
        rows = []
        for x in (first + 2 * pair, first + 2 * pair + 1):
            rows.append(
                jnp.where(
                    position == x - 1,
                    parts[0],
                    jnp.where(position == x, parts[1], jnp.where(position == x + 1, parts[2], 0.0)),
                )
            )
        out_ref[where, row0 + 2 * pair * channels : row0 + 2 * (pair + 1) * channels, :] = jnp.concatenate(
            rows, axis=0
        ).astype(BF16)


def weights_kernel(
    p, w_in, w_mid, w_out, b_mid, b_in, mid_tab, in_tab, pick, row_x, col_tab, m_in, m_out, m_mid, m_back, m_last
):
    for g in range(p.G):
        table = mid_tab[g]
        banded(w_mid[...], table, g * GROUP, GROUP, p.ch, m_mid, g, 0)
        banded(b_mid[...], table, g * GROUP, GROUP, p.ch, m_back, g, 0)
    for g in range(p.GI):
        for t2 in range(p.tl):
            table = in_tab[g, t2]
            banded(w_in[...], table, g * WIDE, WIDE, p.ch, m_in, g, t2 * WIDE * p.ch)
            banded(w_out[...], table, g * WIDE, WIDE, p.ch, m_out, g, t2 * WIDE * p.ch)
        cols = col_tab[g]
        place = one_hot_rows(cols, p.ch)
        position = cols[1:2, :]
        taps = [dot(b_in[b], place).astype(BF16) for b in range(3)]
        for s in range(p.tl):
            x = row_x[g, s]
            total = jnp.zeros((x.shape[0], p.KW), F32)
            for b in range(3):
                total = jnp.where(position == x + (b - 1), dot(pick[g, s], taps[b]), total)
            m_last[g, s] = total.astype(BF16)


def shifted(value, c, ny):
    if c == 1:
        return value
    pieces = []
    for at in range(0, value.shape[1], ny):
        piece = value[:, at : at + ny]
        lane = lax.broadcasted_iota(jnp.int32, piece.shape, 1)
        if c == 0:
            pieces.append(jnp.where(lane == 0, 0.0, pltpu.roll(piece, 1, 1)))
        else:
            pieces.append(jnp.where(lane == ny - 1, 0.0, pltpu.roll(piece, ny - 1, 1)))
    return pieces[0] if len(pieces) == 1 else jnp.concatenate(pieces, axis=1)


def gather_field(p, load, u_ref):
    for f in range(p.F):
        pieces = [load(f, j).reshape(p.R * p.unit, p.ny) for j in range(p.nzb)]
        value = pieces[0] if p.nzb == 1 else jnp.concatenate(pieces, axis=1)
        for c in range(3):
            moved = shifted(value, c, p.ny)
            for g in range(p.GI):
                lo = p.us[g] * p.unit
                start = ((f + 1) * 3 + c) * p.UW
                u_ref[g, start : start + p.UW, :] = moved[lo : lo + p.UW].astype(BF16)


def put_window(p, h_ref, g, t, value):
    for c in range(3):
        moved = shifted(value, c, p.ny).astype(BF16)
        for h in range(p.G):
            lo, hi = max(p.M * g, p.ws[h]), min(p.M * (g + 1), p.ws[h] + p.W)
            if lo < hi:
                start = pl.multiple_of((t + 1) * (3 * p.W) + (c * p.W + lo - p.ws[h]), 16)
                h_ref[h, pl.ds(start, hi - lo), :] = moved[lo - p.M * g : hi - p.M * g]


def first_layer(p, matrix, u_ref, each):
    def body(f, carry):
        for t2 in range(p.tl):
            for g in range(p.G):
                gi, at = g * GROUP // WIDE, g * GROUP % WIDE
                rows = pl.ds(t2 * WIDE * p.ch + at * p.ch, p.M)
                start = pl.multiple_of(f * (3 * p.UW), 16)
                each(f * p.tl + t2, g, dot(matrix[gi, rows, :], u_ref[gi, pl.ds(start, 9 * p.UW), :]))
        return carry

    lax.fori_loop(0, p.F, body, 0)


def middle_layer(p, matrix, h_ref, each):
    def body(t, carry):
        for g in range(p.G):
            start = pl.multiple_of(t * (3 * p.W), 16)
            each(t, g, dot(matrix[g], h_ref[g, pl.ds(start, 9 * p.W), :]))
        return carry

    lax.fori_loop(0, p.T, body, 0)


def last_layer(p, matrix, g_ref, acc_ref):
    acc_ref[...] = jnp.zeros_like(acc_ref)
    size = p.near * p.unit

    def body(f, carry):
        for g in range(p.GI):
            for s in range(p.tl):
                out = dot(matrix[g, s], g_ref[f * p.tl + s, pl.ds(p.ks[g], p.KW), :])
                for target in range(2):
                    slot = f + 1 if target == 0 else (f if s == 0 else f + 2)
                    value = sum(
                        shifted(out[(target * 3 + c) * size : (target * 3 + c + 1) * size], c, p.ny) for c in range(3)
                    )
                    acc_ref[slot, pl.ds(g * size, size), :] += value
        return carry

    lax.fori_loop(0, p.F, body, 0)


def backward(p, zb, load, m_out, m_back, m_last, slope_one, slope_two, back, u_ref, h_ref, g_ref, acc_ref):
    gather_field(p, load, u_ref)

    def after_out(t, g, value):
        rows = pl.ds(p.M * g, p.M)
        put_window(p, h_ref, g, t, slope_two[zb, t, rows, :].astype(F32) * value)

    first_layer(p, m_out, u_ref, after_out)

    def after_mid(t, g, value):
        rows = pl.ds(p.M * g, p.M)
        g_ref[t, rows, :] = (slope_one[zb, t, rows, :].astype(F32) * value).astype(BF16)

    middle_layer(p, m_back, h_ref, after_mid)
    last_layer(p, m_last, g_ref, acc_ref)
    for f in range(p.F):
        for j in range(p.nzb):
            value = acc_ref[f + 1, :, j * p.ny : (j + 1) * p.ny].reshape(p.R, p.unit, p.ny)
            back[:, f, zb * p.nzb + j, :, :] = value.astype(BF16)


def clear_edges(p, u_ref, h_ref):
    u_ref[:, : 3 * p.UW, :] = jnp.zeros((p.GI, 3 * p.UW, p.L), BF16)
    u_ref[:, (p.F + 1) * 3 * p.UW :, :] = jnp.zeros((p.GI, 3 * p.UW, p.L), BF16)
    h_ref[:, : 3 * p.W, :] = jnp.zeros((p.G, 3 * p.W, p.L), BF16)
    h_ref[:, (p.T + 1) * 3 * p.W :, :] = jnp.zeros((p.G, 3 * p.W, p.L), BF16)


def both_kernel(
    p, got, bias_one, bias_two, m_in, m_out, m_mid, m_back, m_last,
    slope_one, slope_two, back, u_ref, h_ref, g_ref, acc_ref,
):
    clear_edges(p, u_ref, h_ref)

    def block(zb, carry):
        def load(which, f, j):
            value = got[:, f, zb * p.nzb + j, :, :].astype(F32)
            return value[:, which * p.unit : (which + 1) * p.unit]

        gather_field(p, functools.partial(load, 0), u_ref)

        def after_in(t, g, value):
            pre = value + bias_one[...]
            sigma = jax.nn.sigmoid(pre)
            slope_one[zb, t, pl.ds(p.M * g, p.M), :] = (sigma * (1.0 + pre * (1.0 - sigma))).astype(BF16)
            put_window(p, h_ref, g, t, pre * sigma)

        first_layer(p, m_in, u_ref, after_in)

        def after_mid(t, g, value):
            pre = value + bias_two[...]
            sigma = jax.nn.sigmoid(pre)
            slope_two[zb, t, pl.ds(p.M * g, p.M), :] = (sigma * (1.0 + pre * (1.0 - sigma))).astype(BF16)

        middle_layer(p, m_mid, h_ref, after_mid)
        backward(
            p, zb, functools.partial(load, 1), m_out, m_back, m_last,
            slope_one, slope_two, back, u_ref, h_ref, g_ref, acc_ref,
        )
        return carry

    lax.fori_loop(0, p.NZB, block, 0)


def back_kernel(
    p, got, before, m_out, m_back, m_last, slope_one, slope_two, back, u_ref, h_ref, g_ref, acc_ref
):
    clear_edges(p, u_ref, h_ref)

    def block(zb, carry):
        def load(f, j):
            at = zb * p.nzb + j
            return got[:, f, at, :, :].astype(F32) - before[:, f, at, :, :].astype(F32)

        backward(p, zb, load, m_out, m_back, m_last, slope_one, slope_two, back, u_ref, h_ref, g_ref, acc_ref)
        return carry

    lax.fori_loop(0, p.NZB, block, 0)


def planes(p):
    for t2 in range(p.tl):
        for part in range(2):
            for x2 in range(p.xl):
                yield (t2 * 2 + part) * p.xl + x2, (part, t2, x2)


def pack_kernel(p, *refs):
    fields, out, scratch = refs[:-2], refs[-2], refs[-1]
    total = len(fields) * p.unit
    for n, field in enumerate(fields):
        for row, at in planes(p):
            scratch[pl.ds(n * p.unit + row, p.nz, stride=total), :] = field[at].T
    out[...] = scratch[...].reshape(p.nz, total, p.ny).astype(BF16)


def less_kernel(p, field, got, out, scratch):
    scratch[...] = got[...].astype(F32).reshape(p.nz * p.unit, p.ny)
    for row, at in planes(p):
        out[at] = field[at] - scratch[pl.ds(row, p.nz, stride=p.unit), :].T


def finish_kernel(p, field, got, first, cotangent, out, gram, scratch):
    scratch[...] = got[...].astype(F32).reshape(p.nz * p.unit, p.ny)
    sums = [jnp.zeros((1, p.nz), F32) for _ in range(3)]
    for row, at in planes(p):
        mapped = field[at] - scratch[pl.ds(row, p.nz, stride=p.unit), :].T
        out[at] = mapped
        old = first[at] - cotangent[at]
        new = mapped - first[at]
        for n, product in enumerate((old * old, new * old, new * new)):
            sums[n] = sums[n] + jnp.sum(product, axis=0, keepdims=True)
    lane = lax.broadcasted_iota(jnp.int32, (1, 128), 1)
    line = jnp.zeros((1, 128), F32)
    for n in range(3):
        line = jnp.where(lane == n, jnp.sum(sums[n], axis=1, keepdims=True), line)
    gram[...] = line


def small_solve(lines, values):
    order = len(values)
    lines = [list(line) for line in lines]
    values = list(values)
    for column in range(order):
        for line in range(column + 1, order):
            factor = lines[line][column] / lines[column][column]
            lines[line] = [a - factor * b for a, b in zip(lines[line], lines[column])]
            values[line] = values[line] - factor * values[column]
    solution = [None] * order
    for line in reversed(range(order)):
        running = values[line]
        for column in range(line + 1, order):
            running = running - lines[line][column] * solution[column]
        solution[line] = running / lines[line][line]
    return solution


def mix_kernel(gathered, first, second, out):
    total = jnp.sum(gathered[...], axis=0)
    g00, g10, g11 = (total[:, n : n + 1] for n in range(3))
    ridge = RIDGE * (g00 + g11) / 2
    one = jnp.ones_like(g00)
    solution = small_solve([[g00 + ridge, g10], [g10, g11 + ridge]], [one, one])
    whole = solution[0] + solution[1]
    alpha = [value / whole for value in solution]
    for part in range(out.shape[0]):
        for t in range(out.shape[1]):
            for x in range(out.shape[2]):
                at = (part, t, x)
                out[at] = alpha[0] * first[at] + alpha[1] * second[at]


def split(value, axis, order):
    high = value.astype(BF16)
    low = (value - high.astype(F32)).astype(BF16)
    return jnp.concatenate([high if kind == "h" else low for kind in order], axis=axis)


def dft_blocks(length, sign, left):
    index = np.arange(length)
    angle = 2.0 * math.pi / length * (index[:, None] * index[None, :] % length)
    cosine, sine = np.cos(angle) / math.sqrt(length), sign * np.sin(angle) / math.sqrt(length)
    if left:
        table = np.block([[cosine, sine], [-sine, cosine]])
    else:
        table = np.block([[cosine, -sine], [sine, cosine]])
    table = table.astype(np.float32)
    high = table.astype(BF16)
    low = (table - high.astype(np.float32)).astype(BF16)
    return np.concatenate([high, high, low], axis=1 if left else 0)


def normal_kernel(field, cotangent, sens, mask, right, left, left_back, right_back, out):
    coils, ny, nz = sens.shape[1], sens.shape[3], sens.shape[4]
    real, imag = field[0, 0, 0], field[1, 0, 0]
    total_real, total_imag = jnp.zeros((ny, nz), F32), jnp.zeros((ny, nz), F32)
    for first in range(0, coils, 2):
        pair = (first, first + 1)
        lines = []
        for c in pair:
            s_real, s_imag = sens[0, c, 0], sens[1, c, 0]
            lines.append(jnp.concatenate([s_real * real - s_imag * imag, s_real * imag + s_imag * real], axis=1))
        value = dot(split(jnp.concatenate(lines, axis=0), 1, "hlh"), right[...])
        value = turn(value, ny, nz)
        value = dot(left[...], split(value, 0, "hlh"))
        keep = jnp.concatenate([mask[0, c].astype(F32) for c in pair], axis=1)
        value = value * jnp.concatenate([keep, keep], axis=0)
        value = dot(left_back[...], split(value, 0, "hlh"))
        value = turn(value, ny, nz)
        value = dot(split(value, 1, "hlh"), right_back[...])
        for n, c in enumerate(pair):
            s_real, s_imag = sens[0, c, 0], sens[1, c, 0]
            z_real, z_imag = value[n * ny : (n + 1) * ny, :nz], value[n * ny : (n + 1) * ny, nz:]
            total_real += s_real * z_real + s_imag * z_imag
            total_imag += s_real * z_imag - s_imag * z_real
    out[0, 0, 0] = cotangent[0, 0, 0] + real - ETA * total_real
    out[1, 0, 0] = cotangent[1, 0, 0] + imag - ETA * total_imag


def turn(value, ny, nz):
    top = jnp.concatenate([value[:ny, :nz], value[ny:, :nz]], axis=1)
    bottom = jnp.concatenate([value[:ny, nz:], value[ny:, nz:]], axis=1)
    return jnp.concatenate([top, bottom], axis=0)


def normal_step(field, cotangent, sensitivity, sampling, tables):
    _, frames, width, ny, nz = field.shape
    coils = sensitivity.shape[1]
    image = pl.BlockSpec((2, 1, 1, ny, nz), lambda x, t: (0, t, x, 0, 0))
    whole = [pl.BlockSpec(table.shape, lambda x, t: (0, 0)) for table in tables]
    return pl.pallas_call(
        normal_kernel,
        grid=(width, frames),
        in_specs=[
            image,
            image,
            pl.BlockSpec((2, coils, 1, ny, nz), lambda x, t: (0, 0, x, 0, 0)),
            pl.BlockSpec((1, coils, ny, nz), lambda x, t: (t, 0, 0, 0)),
            *whole,
        ],
        out_specs=image,
        out_shape=jax.ShapeDtypeStruct(field.shape, F32),
        compiler_params=pltpu.CompilerParams(vmem_limit_bytes=48 << 20),
        cost_estimate=pl.CostEstimate(
            flops=width * frames * coils * 4 * 3 * 2 * 2 * ny * nz * 2 * nz,
            bytes_accessed=20 << 20,
            transcendentals=0,
        ),
        name="normal",
    )(field, cotangent, sensitivity, sampling, *tables)


def call(kernel, outs, args, name, scratch=(), flops=1 << 20, moved=4 << 20):
    shapes = [jax.ShapeDtypeStruct(shape, kind) for shape, kind in outs]
    single = len(shapes) == 1
    return pl.pallas_call(
        kernel,
        in_specs=[VMEM] * len(args),
        out_specs=VMEM if single else [VMEM] * len(shapes),
        out_shape=shapes[0] if single else shapes,
        scratch_shapes=list(scratch),
        compiler_params=pltpu.CompilerParams(vmem_limit_bytes=60 << 20),
        cost_estimate=pl.CostEstimate(flops=flops, bytes_accessed=moved, transcendentals=0),
        name=name,
    )(*args)


def flip_kernel(weight):
    return jnp.transpose(jnp.flip(weight, (2, 3, 4)), (1, 0, 2, 3, 4))


def by_offset(weight):
    outs, ins = weight.shape[:2]
    return jnp.transpose(weight, (3, 0, 2, 4, 1)).reshape(3 * outs, 9 * ins)


def exchange(blocks):
    return lax.all_to_all(blocks, AXES, 0, 0, tiled=True)


def per_device(
    equilibrium, cotangent, sensitivity, sampling, weight_in, bias_in, weight_mid, bias_mid, weight_out
):
    _, frames, width, ny, nz = cotangent.shape
    p = Plan(lax.axis_size("readout"), lax.axis_size("frame"), frames, width, ny, nz, weight_in.shape[0])
    field_shape = cotangent.shape
    z_shape = (p.R, p.F, p.zl, p.unit, ny)
    tables = [
        jnp.asarray(dft_blocks(nz, 1.0, False)),
        jnp.asarray(dft_blocks(ny, 1.0, True)),
        jnp.asarray(dft_blocks(ny, -1.0, True)),
        jnp.asarray(dft_blocks(nz, -1.0, False)),
    ]

    def pack_fields(*fields):
        rows = len(fields) * p.unit
        packed = call(
            functools.partial(pack_kernel, p),
            [((nz, rows, ny), BF16)],
            fields,
            "pack",
            [pltpu.VMEM((nz * rows, ny), F32)],
        )
        return packed.reshape(p.D, p.zl, rows, ny)

    got = exchange(pack_fields(equilibrium, cotangent)).reshape(p.R, p.F, p.zl, 2 * p.unit, ny)

    picks = [[p.out_rows(g, s) for s in range(p.tl)] for g in range(p.GI)]
    back_in = flip_kernel(weight_in)
    last = jnp.transpose(back_in, (3, 2, 4, 0, 1)).reshape(3, 18, p.ch)
    last = jnp.pad(last, ((0, 0), (0, 6), (0, 0)))
    weight_args = [
        by_offset(weight_in),
        by_offset(weight_mid),
        by_offset(flip_kernel(weight_out)),
        by_offset(flip_kernel(weight_mid)),
        last,
        jnp.asarray(np.stack([p.mid_table(g) for g in range(p.G)])),
        jnp.asarray(np.stack([np.stack([p.in_table(g, s) for s in range(p.tl)]) for g in range(p.GI)])),
        jnp.asarray(np.stack([np.stack([pick for pick, _ in line]) for line in picks])),
        jnp.asarray(np.stack([np.stack([x[:, None] for _, x in line]) for line in picks])),
        jnp.asarray(np.stack([p.out_cols(g) for g in range(p.GI)])),
    ]
    in_shape = (p.GI, p.tl * WIDE * p.ch, 9 * p.UW)
    mid_shape = (p.G, p.M, 9 * p.W)
    last_shape = (p.GI, p.tl, 6 * p.near * p.unit, p.KW)
    m_in, m_out, m_mid, m_back, m_last = call(
        functools.partial(weights_kernel, p),
        [(in_shape, BF16), (in_shape, BF16), (mid_shape, BF16), (mid_shape, BF16), (last_shape, BF16)],
        weight_args,
        "weights",
    )
    bias_one = jnp.broadcast_to(jnp.tile(bias_in, GROUP)[:, None], (p.M, p.L))
    bias_two = jnp.broadcast_to(jnp.tile(bias_mid, GROUP)[:, None], (p.M, p.L))

    point = normal_step(cotangent, cotangent, sensitivity, sampling, tables)
    got_point = exchange(pack_fields(point)).reshape(z_shape)

    slope = ((p.NZB, p.T, p.rows, p.L), BF16)
    scratch = [
        pltpu.VMEM((p.GI, (p.F + 2) * 3 * p.UW, p.L), BF16),
        pltpu.VMEM((p.G, (p.T + 2) * 3 * p.W, p.L), BF16),
        pltpu.VMEM((p.T, p.rows, p.L), BF16),
        pltpu.VMEM((p.F + 2, p.R * p.unit, p.L), F32),
    ]
    work = 2 * p.NZB * p.T * p.L * p.rows * 9 * p.W
    slope_one, slope_two, back = call(
        functools.partial(both_kernel, p),
        [slope, slope, (z_shape, BF16)],
        [got, bias_one, bias_two, m_in, m_out, m_mid, m_back, m_last],
        "both",
        scratch,
        3 * work,
        16 << 20,
    )
    returned = exchange(back.reshape(p.D, p.zl, p.unit, ny)).reshape(nz, p.unit, ny)
    back_two = call(
        functools.partial(back_kernel, p),
        [(z_shape, BF16)],
        [got_point, back, m_out, m_back, m_last, slope_one, slope_two],
        "back",
        scratch,
        3 * work // 2,
        12 << 20,
    )
    returned_two = exchange(back_two.reshape(p.D, p.zl, p.unit, ny)).reshape(nz, p.unit, ny)
    turn_scratch = [pltpu.VMEM((nz * p.unit, ny), F32)]
    first = call(
        functools.partial(less_kernel, p), [(field_shape, F32)], [point, returned], "less", turn_scratch
    )
    point_two = normal_step(first, cotangent, sensitivity, sampling, tables)
    second, gram = call(
        functools.partial(finish_kernel, p),
        [(field_shape, F32), ((1, 128), F32)],
        [point_two, returned_two, first, cotangent],
        "finish",
        turn_scratch,
    )
    gathered = exchange(jnp.broadcast_to(gram[None], (p.D, 1, 128)))
    return call(mix_kernel, [(field_shape, F32)], [gathered, first, second], "mix")


def solution(mesh):
    placed = (
        P(None, "frame", "readout", None, None),
        P(None, "frame", "readout", None, None),
        P(None, None, "readout", None, None),
        P("frame", None, None, None),
        P(),
        P(),
        P(),
        P(),
        P(),
    )
    return jax.shard_map(
        per_device,
        mesh=mesh,
        in_specs=placed,
        out_specs=P(None, "frame", "readout", None, None),
        check_vma=False,
    )
```

```python
import functools
import math

import jax
import jax.numpy as jnp
import numpy as np
from jax import lax
from jax.experimental import pallas as pl
from jax.experimental.pallas import tpu as pltpu
from jax.sharding import PartitionSpec as P

ETA = 0.5
RIDGE = 0.0001
AXES = ("readout", "frame")
F32 = jnp.float32
BF16 = jnp.bfloat16
VMEM = pl.BlockSpec(memory_space=pltpu.VMEM)
GROUP = 4
WIDE = 16
LAST = 8


class Plan:
    def __init__(self, devices_x, devices_t, frames, width, ny, nz, channels):
        self.R, self.F, self.tl, self.xl = devices_x, devices_t, frames, width
        self.ny, self.nz, self.ch = ny, nz, channels
        self.D = devices_x * devices_t
        self.T, self.X = frames * devices_t, width * devices_x
        self.zl = nz // self.D
        self.nzb = min(4, self.zl)
        self.NZB = self.zl // self.nzb
        self.L = self.nzb * ny
        self.unit = frames * 2 * width
        self.rows = self.X * channels
        self.M = GROUP * channels
        self.G = self.X // GROUP
        if self.G == 1:
            self.W, self.ws = self.M, [0]
        else:
            self.W = self.M + 32 if self.G == 2 else self.M + 64
            self.ws = [min(max(self.M * g - 32, 0), self.rows - self.W) for g in range(self.G)]
        self.quad = 2 * width
        self.GI = self.X // WIDE
        near = WIDE // width
        extra = 0 if self.GI == 1 else 4
        self.RW = near + extra
        self.UW = self.RW * self.quad
        self.us = [min(max(near * g - extra // 2, 0), devices_x - near - extra) for g in range(self.GI)]
        self.GL = self.X // LAST
        self.near = LAST // width
        wide = LAST * channels
        self.KW = min(wide + (32 if self.GL == 2 else 64), self.rows)
        self.ks = [min(max(wide * g - 32, 0), self.rows - self.KW) for g in range(self.GL)]
        self.part = 6 * self.near * self.unit

    def mid_table(self, g):
        k = np.arange(3 * self.W)
        row = self.ws[g] + k % self.W
        return pack(k // self.W * self.ch + row % self.ch, row // self.ch)

    def in_table(self, g, t2):
        k = np.arange((self.tl + 2) * 3 * self.UW)
        slot, c, rest = k // (3 * self.UW), k // self.UW % 3, k % self.UW
        part, x2, r = rest // (self.xl * self.RW), rest // self.RW % self.xl, self.us[g] + rest % self.RW
        a = slot - t2
        q = np.where((a >= 0) & (a <= 2), (a * 3 + c) * 2 + part, -1)
        return pack(q, r * self.xl + x2)

    def out_rows(self, g, s):
        m = np.arange(2 * 3 * self.near * self.unit)
        target, rest = m // (3 * self.near * self.unit), m % (3 * self.near * self.unit)
        c, rest = rest // (self.near * self.unit), rest % (self.near * self.unit)
        r, rest = self.near * g + rest // self.unit, rest % self.unit
        frame, part, x2 = rest // (2 * self.xl), rest // self.xl % 2, rest % self.xl
        offset = self.tl if s == 0 else -self.tl
        a = s - frame + 1 + np.where(target == 1, offset, 0)
        q = np.where((a >= 0) & (a <= 2), (a * 3 + c) * 2 + part, -1)
        pick = (q[:, None] == np.arange(24)[None, :]).astype(np.float32).astype(BF16)
        return pick, (r * self.xl + x2).astype(np.int32)

    def out_cols(self, g):
        row = self.ks[g] + np.arange(self.KW)
        return pack(row % self.ch, row // self.ch)


def pack(q, position):
    return np.stack([q, position] + [np.zeros_like(q)] * 6).astype(np.int32)


def dot(a, b):
    return jnp.dot(a, b, preferred_element_type=F32)


def one_hot_rows(table, rows, first=0):
    k = table.shape[1]
    index = lax.broadcasted_iota(jnp.int32, (rows, k), 0) + first
    return (index == jnp.broadcast_to(table[0:1, :], (rows, k))).astype(F32).astype(BF16)


def banded(weights, table, first, count, channels, out_ref, where, row0):
    spread = dot(weights, one_hot_rows(table, weights.shape[1]))
    parts = [spread[b * channels : (b + 1) * channels] for b in range(3)]
    position = table[1:2, :]
    for pair in range(count // 2):
        rows = []
        for x in (first + 2 * pair, first + 2 * pair + 1):
            rows.append(
                jnp.where(
                    position == x - 1,
                    parts[0],
                    jnp.where(position == x, parts[1], jnp.where(position == x + 1, parts[2], 0.0)),
                )
            )
        out_ref[where, row0 + 2 * pair * channels : row0 + 2 * (pair + 1) * channels, :] = jnp.concatenate(
            rows, axis=0
        ).astype(BF16)


def banded_taps(raw, flipped, table, first, channels, out_ref, where, scale):
    order = [26 - n if flipped else n for n in range(27)]
    spread = None
    for c in range(3):
        stack = jnp.concatenate([raw[order[ab * 3 + c]].astype(F32) for ab in range(9)], axis=0).astype(BF16)
        part = dot(stack, one_hot_rows(table, channels, c * channels))
        spread = part if spread is None else spread + part
    position = table[1:2, :]
    for a in range(3):
        parts = [spread[(a * 3 + b) * channels : (a * 3 + b + 1) * channels] * scale for b in range(3)]
        for pair in range(GROUP // 2):
            rows = []
            for x in (first + 2 * pair, first + 2 * pair + 1):
                rows.append(
                    jnp.where(
                        position == x - 1,
                        parts[0],
                        jnp.where(position == x, parts[1], jnp.where(position == x + 1, parts[2], 0.0)),
                    )
                )
            at = (a * GROUP + 2 * pair) * channels
            out_ref[where, at : at + 2 * channels, :] = jnp.concatenate(rows, axis=0).astype(BF16)


def weights_kernel(
    p, w_in, w_mid, w_out, b_mid, b_in, mid_tab, in_tab, pick, row_x, col_tab, m_in, m_out, m_mid, m_back, m_last
):
    for g in range(p.G):
        table = mid_tab[g]
        banded_taps(w_mid, False, table, g * GROUP, p.ch, m_mid, g, 0.5)
        banded_taps(b_mid, True, table, g * GROUP, p.ch, m_back, g, 1.0)
    for g in range(p.GI):
        for t2 in range(p.tl):
            table = in_tab[g, t2]
            banded(w_in[...], table, g * WIDE, WIDE, p.ch, m_in, g, t2 * WIDE * p.ch)
            banded(w_out[...], table, g * WIDE, WIDE, p.ch, m_out, g, t2 * WIDE * p.ch)
    for g in range(p.GL):
        cols = col_tab[g]
        place = one_hot_rows(cols, p.ch)
        position = cols[1:2, :]
        taps = [dot(b_in[b], place).astype(BF16) for b in range(3)]
        for s in range(p.tl):
            x = row_x[g, s]
            total = jnp.zeros((x.shape[0], p.KW), F32)
            for b in range(3):
                total = jnp.where(position == x + (b - 1), dot(pick[g, s], taps[b]), total)
            m_last[g, s] = total.astype(BF16)


def shifted(value, c, ny):
    if c == 1:
        return value
    pieces = []
    for at in range(0, value.shape[1], ny):
        piece = value[:, at : at + ny]
        lane = lax.broadcasted_iota(jnp.int32, piece.shape, 1)
        if c == 0:
            pieces.append(jnp.where(lane == 0, jnp.zeros_like(piece), pltpu.roll(piece, 1, 1)))
        else:
            pieces.append(jnp.where(lane == ny - 1, jnp.zeros_like(piece), pltpu.roll(piece, ny - 1, 1)))
    return pieces[0] if len(pieces) == 1 else jnp.concatenate(pieces, axis=1)


def silu_of_half(half):
    double = 1.0 + jnp.tanh(half)
    value = half * double
    sigma = 0.5 * double
    return value, sigma + value * (1.0 - sigma)


def gather_field(p, load, u_ref, row_ref):
    for f in range(p.F):
        for j in range(p.nzb):
            row_ref[f, j] = load(f, j).reshape(p.R * p.unit, p.ny)
        for t2 in range(p.tl):
            lines = []
            for k in range(p.quad):
                start = t2 * p.quad + k
                line = [row_ref[f, j, pl.ds(start, p.R, stride=p.unit), :] for j in range(p.nzb)]
                lines.append(line[0] if p.nzb == 1 else jnp.concatenate(line, axis=1))
            for g in range(p.GI):
                value = jnp.concatenate([line[p.us[g] : p.us[g] + p.RW] for line in lines], axis=0).astype(BF16)
                for c in range(3):
                    start = ((f * p.tl + t2 + 1) * 3 + c) * p.UW
                    u_ref[g, start : start + p.UW, :] = shifted(value, c, p.ny)


def put_window(p, h_ref, g, t, value):
    value = value.astype(BF16)
    for c in range(3):
        moved = shifted(value, c, p.ny)
        for h in range(p.G):
            lo, hi = max(p.M * g, p.ws[h]), min(p.M * (g + 1), p.ws[h] + p.W)
            if lo < hi:
                start = c * p.W + lo - p.ws[h]
                h_ref[h, t, start : start + hi - lo, :] = moved[lo - p.M * g : hi - p.M * g]


def first_layer(p, matrix, u_ref, d_ref, each):
    def issue(f):
        start = pl.multiple_of(f * (p.tl * 3 * p.UW), 16)
        size = (p.tl + 2) * 3 * p.UW
        for gi in range(p.GI):
            d_ref[gi] = dot(matrix[gi], u_ref[gi, pl.ds(start, size), :])

    def finish(f):
        for gi in range(p.GI):
            for t2 in range(p.tl):
                for at in range(WIDE // GROUP):
                    row = (t2 * WIDE + at * GROUP) * p.ch
                    each(f * p.tl + t2, gi * (WIDE // GROUP) + at, d_ref[gi, row : row + p.M, :])

    def body(f, carry):
        finish(f - 1)
        issue(f)
        return carry

    issue(0)
    lax.fori_loop(1, p.F, body, 0)
    finish(p.F - 1)


def middle_layer(p, matrix, h_ref, d_ref, run_ref, each):
    run_ref[...] = jnp.zeros_like(run_ref)

    def issue(t):
        for g in range(p.G):
            d_ref[g] = dot(matrix[g], h_ref[g, t])

    def finish(t):
        for g in range(p.G):
            each(jnp.maximum(t - 1, 0), g, run_ref[g, 0] + d_ref[g, 2 * p.M :, :])
            run_ref[g, 0] = run_ref[g, 1] + d_ref[g, p.M : 2 * p.M, :]
            run_ref[g, 1] = d_ref[g, : p.M, :]

    def body(t, carry):
        finish(t - 1)
        issue(t)
        return carry

    issue(0)
    lax.fori_loop(1, p.T, body, 0)
    finish(p.T - 1)
    for g in range(p.G):
        each(p.T - 1, g, run_ref[g, 0])


def last_layer(p, matrix, g_ref, l_ref, acc_ref):
    acc_ref[...] = jnp.zeros_like(acc_ref)
    size = p.near * p.unit

    def issue(f):
        for g in range(p.GL):
            for s in range(p.tl):
                l_ref[g, s] = dot(matrix[g, s], g_ref[f * p.tl + s, pl.ds(p.ks[g], p.KW), :])

    def finish(f):
        for g in range(p.GL):
            for s in range(p.tl):
                for target in range(2):
                    slot = f + 1 if target == 0 else (f if s == 0 else f + 2)
                    first = target * 3 * size
                    value = l_ref[g, s, first + size : first + 2 * size, :]
                    for c in (0, 2):
                        value = value + shifted(l_ref[g, s, first + c * size : first + (c + 1) * size, :], c, p.ny)
                    acc_ref[slot, pl.ds(g * size, size), :] += value

    def body(f, carry):
        finish(f - 1)
        issue(f)
        return carry

    issue(0)
    lax.fori_loop(1, p.F, body, 0)
    finish(p.F - 1)


def backward(p, zb, load, m_out, m_back, m_last, slope_one, slope_two, back, u_ref, h_ref, g_ref, acc_ref, run_ref, d_ref, e_ref, row_ref, l_ref):
    gather_field(p, load, u_ref, row_ref)

    def after_out(t, g, value):
        rows = pl.ds(p.M * g, p.M)
        put_window(p, h_ref, g, t, slope_two[zb, t, rows, :].astype(F32) * value)

    first_layer(p, m_out, u_ref, d_ref, after_out)

    def after_mid(t, g, value):
        rows = pl.ds(p.M * g, p.M)
        g_ref[t, rows, :] = (slope_one[zb, t, rows, :].astype(F32) * value).astype(BF16)

    middle_layer(p, m_back, h_ref, e_ref, run_ref, after_mid)
    last_layer(p, m_last, g_ref, l_ref, acc_ref)
    for f in range(p.F):
        for j in range(p.nzb):
            value = acc_ref[f + 1, :, j * p.ny : (j + 1) * p.ny].reshape(p.R, p.unit, p.ny)
            back[:, f, zb * p.nzb + j, :, :] = value.astype(BF16)


def clear_edges(p, u_ref):
    u_ref[:, : 3 * p.UW, :] = jnp.zeros((p.GI, 3 * p.UW, p.L), BF16)
    u_ref[:, (p.T + 1) * 3 * p.UW :, :] = jnp.zeros((p.GI, 3 * p.UW, p.L), BF16)


def both_kernel(
    p, got, bias_one, bias_two, m_in, m_out, m_mid, m_back, m_last,
    slope_one, slope_two, back, u_ref, h_ref, g_ref, acc_ref, run_ref, d_ref, e_ref, row_ref, l_ref,
):
    clear_edges(p, u_ref)

    def block(zb, carry):
        def load(which, f, j):
            value = got[:, f, zb * p.nzb + j, :, :].astype(F32)
            return value[:, which * p.unit : (which + 1) * p.unit]

        gather_field(p, functools.partial(load, 0), u_ref, row_ref)

        def after_in(t, g, value):
            hidden, slope = silu_of_half(value + bias_one[...])
            slope_one[zb, t, pl.ds(p.M * g, p.M), :] = slope.astype(BF16)
            put_window(p, h_ref, g, t, hidden)

        first_layer(p, m_in, u_ref, d_ref, after_in)

        def after_mid(t, g, value):
            _, slope = silu_of_half(value + bias_two[...])
            slope_two[zb, t, pl.ds(p.M * g, p.M), :] = slope.astype(BF16)

        middle_layer(p, m_mid, h_ref, e_ref, run_ref, after_mid)
        backward(
            p, zb, functools.partial(load, 1), m_out, m_back, m_last,
            slope_one, slope_two, back, u_ref, h_ref, g_ref, acc_ref, run_ref, d_ref, e_ref, row_ref, l_ref,
        )
        return carry

    lax.fori_loop(0, p.NZB, block, 0)


def back_kernel(
    p, got, before, m_out, m_back, m_last, slope_one, slope_two, back, u_ref, h_ref, g_ref, acc_ref, run_ref, d_ref, e_ref, row_ref, l_ref
):
    clear_edges(p, u_ref)

    def block(zb, carry):
        def load(f, j):
            at = zb * p.nzb + j
            return got[:, f, at, :, :].astype(F32) - before[:, f, at, :, :].astype(F32)

        backward(p, zb, load, m_out, m_back, m_last, slope_one, slope_two, back, u_ref, h_ref, g_ref, acc_ref, run_ref, d_ref, e_ref, row_ref, l_ref)
        return carry

    lax.fori_loop(0, p.NZB, block, 0)


def planes(p):
    for t2 in range(p.tl):
        for part in range(2):
            for x2 in range(p.xl):
                yield (t2 * 2 + part) * p.xl + x2, (part, t2, x2)


def pack_kernel(p, equilibrium, cotangent, out, turned, scratch):
    total = 2 * p.unit
    for row, at in planes(p):
        scratch[pl.ds(row, p.nz, stride=total), :] = equilibrium[at].T
        plane = cotangent[at].T
        turned[at] = plane
        scratch[pl.ds(p.unit + row, p.nz, stride=total), :] = plane
    out[...] = scratch[...].reshape(p.nz, total, p.ny).astype(BF16)


def finish_kernel(p, field, got, first, cotangent, out, gram, scratch):
    scratch[...] = got[...].astype(F32).reshape(p.nz * p.unit, p.ny)
    sums = [jnp.zeros((1, p.ny), F32) for _ in range(3)]
    for row, at in planes(p):
        mapped = field[at] - scratch[pl.ds(row, p.nz, stride=p.unit), :]
        out[at] = mapped
        old = first[at] - cotangent[at]
        new = mapped - first[at]
        for n, product in enumerate((old * old, new * old, new * new)):
            sums[n] = sums[n] + jnp.sum(product, axis=0, keepdims=True)
    lane = lax.broadcasted_iota(jnp.int32, (1, 128), 1)
    line = jnp.zeros((1, 128), F32)
    for n in range(3):
        line = jnp.where(lane == n, jnp.sum(sums[n], axis=1, keepdims=True), line)
    gram[...] = jnp.broadcast_to(line[None], gram.shape)


def small_solve(lines, values):
    order = len(values)
    lines = [list(line) for line in lines]
    values = list(values)
    for column in range(order):
        for line in range(column + 1, order):
            factor = lines[line][column] / lines[column][column]
            lines[line] = [a - factor * b for a, b in zip(lines[line], lines[column])]
            values[line] = values[line] - factor * values[column]
    solution = [None] * order
    for line in reversed(range(order)):
        running = values[line]
        for column in range(line + 1, order):
            running = running - lines[line][column] * solution[column]
        solution[line] = running / lines[line][line]
    return solution


def mix_kernel(gathered, first, second, out):
    total = jnp.sum(gathered[...], axis=0)
    g00, g10, g11 = (total[:, n : n + 1] for n in range(3))
    ridge = RIDGE * (g00 + g11) / 2
    one = jnp.ones_like(g00)
    solution = small_solve([[g00 + ridge, g10], [g10, g11 + ridge]], [one, one])
    whole = solution[0] + solution[1]
    alpha = [value / whole for value in solution]
    for part in range(out.shape[0]):
        for t in range(out.shape[1]):
            for x in range(out.shape[2]):
                at = (part, t, x)
                out[at] = (alpha[0] * first[at] + alpha[1] * second[at]).T


def dft_table(length, sign):
    index = np.arange(length)
    angle = 2.0 * math.pi / length * (index[:, None] * index[None, :] % length)
    cosine, sine = np.cos(angle) / math.sqrt(length), sign * np.sin(angle) / math.sqrt(length)
    table = np.block([[cosine, -sine], [sine, cosine]]).astype(np.float32)
    high = table.astype(BF16)
    low = (table - high.astype(np.float32)).astype(BF16)
    return np.concatenate([high, high, low], axis=0)


def transform(value, table):
    high = value.astype(BF16)
    low = (value - high.astype(F32)).astype(BF16)
    return dot(jnp.concatenate([high, low, high], axis=1), table[...])


def turned_images(value, count, rows, columns):
    images = []
    for n in range(count):
        image = value[n * rows : (n + 1) * rows]
        images.append(jnp.concatenate([image[:, :columns].T, image[:, columns:].T], axis=1))
    return jnp.concatenate(images, axis=0)


def normal_sum(real, imag, sens, mask, tables):
    forward_y, forward_z, inverse_z, inverse_y = tables
    coils, nz, ny = sens.shape[1], sens.shape[3], sens.shape[4]
    total_real, total_imag = jnp.zeros((nz, ny), F32), jnp.zeros((nz, ny), F32)
    count = math.gcd(coils, 4)
    groups = [range(first, first + count) for first in range(0, coils, count)]
    values, keeps = [], []
    for group in groups:
        lines, keep = [], []
        for c in group:
            s_real, s_imag = sens[0, c, 0], sens[1, c, 0]
            lines.append(jnp.concatenate([s_real * real - s_imag * imag, s_real * imag + s_imag * real], axis=1))
            line = mask[0, c].astype(F32)
            keep.append(jnp.concatenate([line, line], axis=1))
        values.append(jnp.concatenate(lines, axis=0))
        keeps.append(jnp.concatenate(keep, axis=0))
    values = [transform(value, forward_y) for value in values]
    values = [transform(turned_images(value, count, nz, ny), forward_z) for value in values]
    values = [transform(value * keep, inverse_z) for value, keep in zip(values, keeps)]
    values = [transform(turned_images(value, count, ny, nz), inverse_y) for value in values]
    for group, value in zip(groups, values):
        for n, c in enumerate(group):
            s_real, s_imag = sens[0, c, 0], sens[1, c, 0]
            z_real, z_imag = value[n * nz : (n + 1) * nz, :ny], value[n * nz : (n + 1) * nz, ny:]
            total_real += s_real * z_real + s_imag * z_imag
            total_imag += s_real * z_imag - s_imag * z_real
    return total_real, total_imag


def first_normal_kernel(
    p, cotangent, sens, mask, forward_y, forward_z, inverse_z, inverse_y, point, turned, packed, scratch
):
    x, t = pl.program_id(0), pl.program_id(1)

    @pl.when(t == 0)
    def _():
        for part in range(2):
            for c in range(sens.shape[1]):
                turned[part, c, 0] = sens[part, c, 0].T

    real, imag = cotangent[0, 0, 0], cotangent[1, 0, 0]
    sums = normal_sum(real, imag, turned, mask, (forward_y, forward_z, inverse_z, inverse_y))
    for part, (value, total) in enumerate(zip((real, imag), sums)):
        value = value + value - ETA * total
        point[part, 0, 0] = value
        scratch[pl.ds((t * 2 + part) * p.xl + x, p.nz, stride=p.unit), :] = value

    @pl.when((x == p.xl - 1) & (t == p.tl - 1))
    def _():
        packed[...] = scratch[...].reshape(p.nz, p.unit, p.ny).astype(BF16)


def next_normal_kernel(
    p, point, returned, cotangent, sens, mask, forward_y, forward_z, inverse_z, inverse_y, field, out, scratch
):
    x, t = pl.program_id(0), pl.program_id(1)

    @pl.when((x == 0) & (t == 0))
    def _():
        scratch[...] = returned[...].astype(F32).reshape(p.nz * p.unit, p.ny)

    values = []
    for part in range(2):
        plane = scratch[pl.ds((t * 2 + part) * p.xl + x, p.nz, stride=p.unit), :]
        values.append(point[part, 0, 0] - plane)
        field[part, 0, 0] = values[part]
    sums = normal_sum(values[0], values[1], sens, mask, (forward_y, forward_z, inverse_z, inverse_y))
    for part, (value, total) in enumerate(zip(values, sums)):
        out[part, 0, 0] = cotangent[part, 0, 0] + value - ETA * total


def normal_call(p, kernel, args, specs, outs, out_specs, name, coils):
    return pl.pallas_call(
        functools.partial(kernel, p),
        grid=(p.xl, p.tl),
        in_specs=specs,
        out_specs=out_specs,
        out_shape=[jax.ShapeDtypeStruct(shape, kind) for shape, kind in outs],
        scratch_shapes=[pltpu.VMEM((p.nz * p.unit, p.ny), F32)],
        compiler_params=pltpu.CompilerParams(vmem_limit_bytes=48 << 20),
        cost_estimate=pl.CostEstimate(
            flops=p.xl * p.tl * coils * 4 * 3 * 2 * 2 * p.ny * p.nz * 2 * p.nz,
            bytes_accessed=20 << 20,
            transcendentals=0,
        ),
        name=name,
    )(*args)


def call(kernel, outs, args, name, scratch=(), flops=1 << 20, moved=4 << 20):
    shapes = [jax.ShapeDtypeStruct(shape, kind) for shape, kind in outs]
    single = len(shapes) == 1
    return pl.pallas_call(
        kernel,
        in_specs=[VMEM] * len(args),
        out_specs=VMEM if single else [VMEM] * len(shapes),
        out_shape=shapes[0] if single else shapes,
        scratch_shapes=list(scratch),
        compiler_params=pltpu.CompilerParams(vmem_limit_bytes=60 << 20),
        cost_estimate=pl.CostEstimate(flops=flops, bytes_accessed=moved, transcendentals=0),
        name=name,
    )(*args)


def flip_kernel(weight):
    return jnp.transpose(jnp.flip(weight, (2, 3, 4)), (1, 0, 2, 3, 4))


def by_offset(weight):
    outs, ins = weight.shape[:2]
    return jnp.transpose(weight, (3, 0, 2, 4, 1)).reshape(3 * outs, 9 * ins)


def exchange(blocks):
    return lax.all_to_all(blocks, AXES, 0, 0, tiled=True)


def per_device(
    equilibrium, cotangent, sensitivity, sampling, weight_in, bias_in, weight_mid, bias_mid, weight_out
):
    _, frames, width, ny, nz = cotangent.shape
    p = Plan(lax.axis_size("readout"), lax.axis_size("frame"), frames, width, ny, nz, weight_in.shape[0])
    coils = sensitivity.shape[1]
    turned_shape = (2, frames, width, nz, ny)
    z_shape = (p.R, p.F, p.zl, p.unit, ny)
    tables = [
        jnp.asarray(dft_table(ny, 1.0)),
        jnp.asarray(dft_table(nz, 1.0)),
        jnp.asarray(dft_table(nz, -1.0)),
        jnp.asarray(dft_table(ny, -1.0)),
    ]
    if ny == nz:
        tables[1], tables[3] = tables[0], tables[2]
    image = pl.BlockSpec((2, 1, 1, nz, ny), lambda x, t: (0, t, x, 0, 0))
    lines = pl.BlockSpec((nz, p.unit, ny), lambda x, t: (0, 0, 0))
    maps = pl.BlockSpec((2, coils, 1, ny, nz), lambda x, t: (0, 0, x, 0, 0))
    turned_maps = pl.BlockSpec((2, coils, 1, nz, ny), lambda x, t: (0, 0, x, 0, 0))
    masks = pl.BlockSpec((1, coils, ny, nz), lambda x, t: (t, 0, 0, 0))
    whole = [pl.BlockSpec(table.shape, lambda x, t: (0, 0)) for table in tables]

    packed, turned = call(
        functools.partial(pack_kernel, p),
        [((nz, 2 * p.unit, ny), BF16), (turned_shape, F32)],
        (equilibrium, cotangent),
        "pack",
        [pltpu.VMEM((nz * 2 * p.unit, ny), F32)],
    )
    got = exchange(packed.reshape(p.D, p.zl, 2 * p.unit, ny)).reshape(p.R, p.F, p.zl, 2 * p.unit, ny)

    picks = [[p.out_rows(g, s) for s in range(p.tl)] for g in range(p.GL)]
    back_in = flip_kernel(weight_in)
    last = jnp.transpose(back_in, (3, 2, 4, 0, 1)).reshape(3, 18, p.ch)
    last = jnp.pad(last, ((0, 0), (0, 6), (0, 0)))
    weight_args = [
        by_offset(weight_in) * jnp.asarray(0.5, BF16),
        jnp.transpose(weight_mid, (2, 3, 4, 0, 1)).reshape(27, p.ch, p.ch),
        by_offset(flip_kernel(weight_out)),
        jnp.transpose(weight_mid, (2, 3, 4, 1, 0)).reshape(27, p.ch, p.ch),
        last,
        jnp.asarray(np.stack([p.mid_table(g) for g in range(p.G)])),
        jnp.asarray(np.stack([np.stack([p.in_table(g, s) for s in range(p.tl)]) for g in range(p.GI)])),
        jnp.asarray(np.stack([np.stack([pick for pick, _ in line]) for line in picks])),
        jnp.asarray(np.stack([np.stack([x[:, None] for _, x in line]) for line in picks])),
        jnp.asarray(np.stack([p.out_cols(g) for g in range(p.GL)])),
    ]
    in_shape = (p.GI, p.tl * WIDE * p.ch, (p.tl + 2) * 3 * p.UW)
    mid_shape = (p.G, 3 * p.M, 3 * p.W)
    last_shape = (p.GL, p.tl, p.part, p.KW)
    m_in, m_out, m_mid, m_back, m_last = call(
        functools.partial(weights_kernel, p),
        [(in_shape, BF16), (in_shape, BF16), (mid_shape, BF16), (mid_shape, BF16), (last_shape, BF16)],
        weight_args,
        "weights",
    )
    bias_one = jnp.broadcast_to(jnp.tile(0.5 * bias_in, GROUP)[:, None], (p.M, p.L))
    bias_two = jnp.broadcast_to(jnp.tile(0.5 * bias_mid, GROUP)[:, None], (p.M, p.L))

    point, turned_sens, packed = normal_call(
        p,
        first_normal_kernel,
        [turned, sensitivity, sampling, *tables],
        [image, maps, masks, *whole],
        [(turned_shape, F32), ((2, coils, width, nz, ny), F32), ((nz, p.unit, ny), BF16)],
        [image, turned_maps, lines],
        "normal_one",
        coils,
    )
    got_point = exchange(packed.reshape(p.D, p.zl, p.unit, ny)).reshape(z_shape)

    slope = ((p.NZB, p.T, p.rows, p.L), BF16)
    scratch = [
        pltpu.VMEM((p.GI, (p.T + 2) * 3 * p.UW, p.L), BF16),
        pltpu.VMEM((p.G, p.T, 3 * p.W, p.L), BF16),
        pltpu.VMEM((p.T, p.rows, p.L), BF16),
        pltpu.VMEM((p.F + 2, p.R * p.unit, p.L), F32),
        pltpu.VMEM((p.G, 2, p.M, p.L), F32),
        pltpu.VMEM((p.GI, p.tl * WIDE * p.ch, p.L), F32),
        pltpu.VMEM((p.G, 3 * p.M, p.L), F32),
        pltpu.VMEM((p.F, p.nzb, p.R * p.unit, ny), F32),
        pltpu.VMEM((p.GL, p.tl, p.part, p.L), F32),
    ]
    work = 2 * p.NZB * p.T * p.L * p.rows * 9 * p.W
    slope_one, slope_two, back = call(
        functools.partial(both_kernel, p),
        [slope, slope, (z_shape, BF16)],
        [got, bias_one, bias_two, m_in, m_out, m_mid, m_back, m_last],
        "both",
        scratch,
        3 * work,
        16 << 20,
    )
    returned = exchange(back.reshape(p.D, p.zl, p.unit, ny)).reshape(nz, p.unit, ny)
    back_two = call(
        functools.partial(back_kernel, p),
        [(z_shape, BF16)],
        [got_point, back, m_out, m_back, m_last, slope_one, slope_two],
        "back",
        scratch,
        3 * work // 2,
        12 << 20,
    )
    returned_two = exchange(back_two.reshape(p.D, p.zl, p.unit, ny)).reshape(nz, p.unit, ny)
    first, point_two = normal_call(
        p,
        next_normal_kernel,
        [point, returned, turned, turned_sens, sampling, *tables],
        [image, lines, image, turned_maps, masks, *whole],
        [(turned_shape, F32), (turned_shape, F32)],
        [image, image],
        "normal_two",
        coils,
    )
    second, gram = call(
        functools.partial(finish_kernel, p),
        [(turned_shape, F32), ((p.D, 1, 128), F32)],
        [point_two, returned_two, first, turned],
        "finish",
        [pltpu.VMEM((nz * p.unit, ny), F32)],
    )
    return call(mix_kernel, [(cotangent.shape, F32)], [exchange(gram), first, second], "mix")


def solution(mesh):
    placed = (
        P(None, "frame", "readout", None, None),
        P(None, "frame", "readout", None, None),
        P(None, None, "readout", None, None),
        P("frame", None, None, None),
        P(),
        P(),
        P(),
        P(),
        P(),
    )
    return jax.shard_map(
        per_device,
        mesh=mesh,
        in_specs=placed,
        out_specs=P(None, "frame", "readout", None, None),
        check_vma=False,
    )
```

```python
import functools
import math

import jax
import jax.numpy as jnp
import numpy as np
from jax import lax
from jax.experimental import pallas as pl
from jax.experimental.pallas import tpu as pltpu
from jax.sharding import PartitionSpec as P

ETA = 0.5
RIDGE = 0.0001
AXES = ("readout", "frame")
F32 = jnp.float32
BF16 = jnp.bfloat16
VMEM = pl.BlockSpec(memory_space=pltpu.VMEM)
ANY = pl.BlockSpec(memory_space=pl.ANY)
GROUP = 4
WIDE = 16
LAST = 8


class Plan:
    def __init__(self, devices_x, devices_t, frames, width, ny, nz, channels):
        self.R, self.F, self.tl, self.xl = devices_x, devices_t, frames, width
        self.ny, self.nz, self.ch = ny, nz, channels
        self.D = devices_x * devices_t
        self.T, self.X = frames * devices_t, width * devices_x
        self.zl = nz // self.D
        self.nzb = min(4, self.zl)
        self.NZB = self.zl // self.nzb
        self.L = self.nzb * ny
        self.unit = frames * 2 * width
        self.rows = self.X * channels
        self.M = GROUP * channels
        self.G = self.X // GROUP
        if self.G == 1:
            self.W, self.ws = self.M, [0]
        else:
            self.W = self.M + 32 if self.G == 2 else self.M + 64
            self.ws = [min(max(self.M * g - 32, 0), self.rows - self.W) for g in range(self.G)]
        self.quad = 2 * width
        self.GI = self.X // WIDE
        near = WIDE // width
        extra = 0 if self.GI == 1 else 4
        self.RW = near + extra
        self.UW = self.RW * self.quad
        self.us = [min(max(near * g - extra // 2, 0), devices_x - near - extra) for g in range(self.GI)]
        self.GL = self.X // LAST
        self.near = LAST // width
        wide = LAST * channels
        self.KW = min(wide + (32 if self.GL == 2 else 64), self.rows)
        self.ks = [min(max(wide * g - 32, 0), self.rows - self.KW) for g in range(self.GL)]
        self.part = 6 * self.near * self.unit

    def mid_of(self, g):
        offsets = [self.ws[n] - self.M * n for n in range(self.G)]
        return sorted(set(offsets), reverse=True).index(offsets[g])

    def mid_first(self):
        return [next(g for g in range(self.G) if self.mid_of(g) == n) for n in range(self.mid_of(self.G - 1) + 1)]

    def mid_table(self, g):
        k = np.arange(3 * self.W)
        row = self.ws[g] + k % self.W
        return pack(k // self.W * self.ch + row % self.ch, row // self.ch)

    def in_table(self, g, t2):
        k = np.arange((self.tl + 2) * 3 * self.UW)
        slot, c, rest = k // (3 * self.UW), k // self.UW % 3, k % self.UW
        part, x2, r = rest // (self.xl * self.RW), rest // self.RW % self.xl, self.us[g] + rest % self.RW
        a = slot - t2
        q = np.where((a >= 0) & (a <= 2), (a * 3 + c) * 2 + part, -1)
        return pack(q, r * self.xl + x2)

    def out_rows(self, g, s):
        m = np.arange(2 * 3 * self.near * self.unit)
        target, rest = m // (3 * self.near * self.unit), m % (3 * self.near * self.unit)
        c, rest = rest // (self.near * self.unit), rest % (self.near * self.unit)
        r, rest = self.near * g + rest // self.unit, rest % self.unit
        frame, part, x2 = rest // (2 * self.xl), rest // self.xl % 2, rest % self.xl
        offset = self.tl if s == 0 else -self.tl
        a = s - frame + 1 + np.where(target == 1, offset, 0)
        q = np.where((a >= 0) & (a <= 2), (a * 3 + c) * 2 + part, -1)
        pick = (q[:, None] == np.arange(24)[None, :]).astype(np.float32).astype(BF16)
        return pick, (r * self.xl + x2).astype(np.int32)

    def out_cols(self, g):
        row = self.ks[g] + np.arange(self.KW)
        return pack(row % self.ch, row // self.ch)


def pack(q, position):
    return np.stack([q, position] + [np.zeros_like(q)] * 6).astype(np.int32)


def dot(a, b):
    return jnp.dot(a, b, preferred_element_type=F32)


def one_hot_rows(table, rows, first=0):
    k = table.shape[1]
    index = lax.broadcasted_iota(jnp.int32, (rows, k), 0) + first
    return (index == jnp.broadcast_to(table[0:1, :], (rows, k))).astype(F32).astype(BF16)


def banded(weights, table, first, count, channels, out_ref, where, row0):
    spread = dot(weights, one_hot_rows(table, weights.shape[1]))
    parts = [spread[b * channels : (b + 1) * channels] for b in range(3)]
    position = table[1:2, :]
    for pair in range(count // 2):
        rows = []
        for x in (first + 2 * pair, first + 2 * pair + 1):
            rows.append(
                jnp.where(
                    position == x - 1,
                    parts[0],
                    jnp.where(position == x, parts[1], jnp.where(position == x + 1, parts[2], 0.0)),
                )
            )
        out_ref[where, row0 + 2 * pair * channels : row0 + 2 * (pair + 1) * channels, :] = jnp.concatenate(
            rows, axis=0
        ).astype(BF16)


def banded_taps(raw, flipped, table, first, channels, out_ref, where, scale):
    order = [26 - n if flipped else n for n in range(27)]
    spread = None
    for c in range(3):
        stack = jnp.concatenate([raw[order[ab * 3 + c]].astype(F32) for ab in range(9)], axis=0).astype(BF16)
        part = dot(stack, one_hot_rows(table, channels, c * channels))
        spread = part if spread is None else spread + part
    position = table[1:2, :]
    for a in range(3):
        parts = [spread[(a * 3 + b) * channels : (a * 3 + b + 1) * channels] * scale for b in range(3)]
        for pair in range(GROUP // 2):
            rows = []
            for x in (first + 2 * pair, first + 2 * pair + 1):
                rows.append(
                    jnp.where(
                        position == x - 1,
                        parts[0],
                        jnp.where(position == x, parts[1], jnp.where(position == x + 1, parts[2], 0.0)),
                    )
                )
            at = (a * GROUP + 2 * pair) * channels
            out_ref[where, at : at + 2 * channels, :] = jnp.concatenate(rows, axis=0).astype(BF16)


def weights_kernel(
    p, w_in, w_mid, w_out, b_mid, b_in, one, two, mid_tab, in_tab, pick, row_x, col_tab,
    m_in, m_out, m_mid, m_back, m_last, bias_one, bias_two,
):
    for line, out in ((one, bias_one), (two, bias_two)):
        shape = (p.ch, p.ch)
        same = lax.broadcasted_iota(jnp.int32, shape, 0) == lax.broadcasted_iota(jnp.int32, shape, 1)
        column = 0.5 * jnp.sum(jnp.where(same, line[...], 0.0), axis=1, keepdims=True)
        for n in range(GROUP):
            out[n * p.ch : (n + 1) * p.ch, :] = jnp.broadcast_to(column, (p.ch, p.L))
    for n, g in enumerate(p.mid_first()):
        table = mid_tab[n]
        banded_taps(w_mid, False, table, g * GROUP, p.ch, m_mid, n, 0.5)
        banded_taps(b_mid, True, table, g * GROUP, p.ch, m_back, n, 1.0)
    for g in range(p.GI):
        for t2 in range(p.tl):
            table = in_tab[g, t2]
            banded(w_in[...], table, g * WIDE, WIDE, p.ch, m_in, g, t2 * WIDE * p.ch)
            banded(w_out[...], table, g * WIDE, WIDE, p.ch, m_out, g, t2 * WIDE * p.ch)
    for g in range(p.GL):
        cols = col_tab[g]
        place = one_hot_rows(cols, p.ch)
        position = cols[1:2, :]
        taps = [dot(b_in[b], place).astype(BF16) for b in range(3)]
        for s in range(p.tl):
            x = row_x[g, s]
            total = jnp.zeros((x.shape[0], p.KW), F32)
            for b in range(3):
                total = jnp.where(position == x + (b - 1), dot(pick[g, s], taps[b]), total)
            m_last[g, s] = total.astype(BF16)


def shifted(value, c, ny):
    if c == 1:
        return value
    pieces = []
    for at in range(0, value.shape[1], ny):
        piece = value[:, at : at + ny]
        lane = lax.broadcasted_iota(jnp.int32, piece.shape, 1)
        if c == 0:
            pieces.append(jnp.where(lane == 0, jnp.zeros_like(piece), pltpu.roll(piece, 1, 1)))
        else:
            pieces.append(jnp.where(lane == ny - 1, jnp.zeros_like(piece), pltpu.roll(piece, ny - 1, 1)))
    return pieces[0] if len(pieces) == 1 else jnp.concatenate(pieces, axis=1)


def silu_of_half(half):
    double = 1.0 + jnp.tanh(half)
    value = half * double
    sigma = 0.5 * double
    return value, sigma + value * (1.0 - sigma)


def gather_field(p, load, u_ref, row_ref):
    for f in range(p.F):
        for j in range(p.nzb):
            row_ref[f, j] = load(f, j).reshape(p.R * p.unit, p.ny)
        for t2 in range(p.tl):
            lines = []
            for k in range(p.quad):
                start = t2 * p.quad + k
                line = [row_ref[f, j, pl.ds(start, p.R, stride=p.unit), :] for j in range(p.nzb)]
                lines.append(line[0] if p.nzb == 1 else jnp.concatenate(line, axis=1))
            for g in range(p.GI):
                value = jnp.concatenate([line[p.us[g] : p.us[g] + p.RW] for line in lines], axis=0).astype(BF16)
                for c in range(3):
                    start = ((f * p.tl + t2 + 1) * 3 + c) * p.UW
                    u_ref[g, start : start + p.UW, :] = shifted(value, c, p.ny)


def put_window(p, h_ref, g, t, value):
    value = value.astype(BF16)
    for c in range(3):
        moved = shifted(value, c, p.ny)
        for h in range(p.G):
            lo, hi = max(p.M * g, p.ws[h]), min(p.M * (g + 1), p.ws[h] + p.W)
            if lo < hi:
                start = c * p.W + lo - p.ws[h]
                h_ref[h, t, start : start + hi - lo, :] = moved[lo - p.M * g : hi - p.M * g]


class Layer:
    def __init__(self, steps, issue, finish, end=None):
        self.steps, self.issue, self.finish, self.end = steps, issue, finish, end

    def start(self):
        self.issue(0)

    def run(self, ahead=None):
        def body(n, carry):
            self.finish(n - 1)
            self.issue(n)
            return carry

        lax.fori_loop(1, self.steps, body, 0)
        if ahead is not None:
            ahead()
        self.finish(self.steps - 1)
        if self.end is not None:
            self.end()


def first_layer(p, matrix, u_ref, d_ref, each):
    def issue(f):
        start = f * (p.tl * 3 * p.UW)
        if not isinstance(f, int):
            start = pl.multiple_of(start, 16)
        size = (p.tl + 2) * 3 * p.UW
        for gi in range(p.GI):
            d_ref[gi] = dot(matrix[gi], u_ref[gi, pl.ds(start, size), :])

    def finish(f):
        for gi in range(p.GI):
            for t2 in range(p.tl):
                for at in range(WIDE // GROUP):
                    row = (t2 * WIDE + at * GROUP) * p.ch
                    each(f * p.tl + t2, gi * (WIDE // GROUP) + at, d_ref[gi, row : row + p.M, :])

    return Layer(p.F, issue, finish)


def middle_layer(p, matrix, h_ref, d_ref, run_ref, each):
    def issue(t):
        if isinstance(t, int):
            run_ref[...] = jnp.zeros_like(run_ref)
        for g in range(p.G):
            d_ref[g] = dot(matrix[p.mid_of(g)], h_ref[g, t])

    def finish(t):
        for g in range(p.G):
            before = jnp.maximum(t - 1, 0) if not isinstance(t, int) else t - 1
            each(before, g, run_ref[g, 0] + d_ref[g, 2 * p.M :, :])
            run_ref[g, 0] = run_ref[g, 1] + d_ref[g, p.M : 2 * p.M, :]
            run_ref[g, 1] = d_ref[g, : p.M, :]

    def end():
        for g in range(p.G):
            each(p.T - 1, g, run_ref[g, 0])

    return Layer(p.T, issue, finish, end)


def last_layer(p, matrix, g_ref, l_ref, acc_ref):
    size = p.near * p.unit

    def issue(f):
        if isinstance(f, int):
            acc_ref[...] = jnp.zeros_like(acc_ref)
        for g in range(p.GL):
            for s in range(p.tl):
                l_ref[g, s] = dot(matrix[g, s], g_ref[f * p.tl + s, pl.ds(p.ks[g], p.KW), :])

    def finish(f):
        for g in range(p.GL):
            for s in range(p.tl):
                for target in range(2):
                    slot = f + 1 if target == 0 else (f if s == 0 else f + 2)
                    first = target * 3 * size
                    value = l_ref[g, s, first + size : first + 2 * size, :]
                    for c in (0, 2):
                        value = value + shifted(l_ref[g, s, first + c * size : first + (c + 1) * size, :], c, p.ny)
                    acc_ref[slot, pl.ds(g * size, size), :] += value

    return Layer(p.F, issue, finish)


def backward(p, load, m_out, m_back, m_last, slope_one, slope_two, put, scratch):
    u_ref, h_ref, g_ref, acc_ref, run_ref, d_ref, e_ref, row_ref, l_ref = scratch

    def after_out(t, g, value):
        rows = pl.ds(p.M * g, p.M)
        put_window(p, h_ref, g, t, slope_two[t, rows, :].astype(F32) * value)

    def after_mid(t, g, value):
        rows = pl.ds(p.M * g, p.M)
        g_ref[t, rows, :] = (slope_one[t, rows, :].astype(F32) * value).astype(BF16)

    out = first_layer(p, m_out, u_ref, d_ref, after_out)
    middle = middle_layer(p, m_back, h_ref, e_ref, run_ref, after_mid)
    last = last_layer(p, m_last, g_ref, l_ref, acc_ref)

    def begin():
        gather_field(p, load, u_ref, row_ref)
        out.start()

    def rest(before_two, before_one):
        before_two()

        def ahead():
            before_one()
            middle.start()

        out.run(ahead)
        middle.run(last.start)
        last.run()
        for f in range(p.F):
            for j in range(p.nzb):
                value = acc_ref[f + 1, :, j * p.ny : (j + 1) * p.ny].reshape(p.R, p.unit, p.ny)
                put(f, j, value.astype(BF16))

    return begin, rest


def clear_edges(p, u_ref):
    u_ref[:, : 3 * p.UW, :] = jnp.zeros((p.GI, 3 * p.UW, p.L), BF16)
    u_ref[:, (p.T + 1) * 3 * p.UW :, :] = jnp.zeros((p.GI, 3 * p.UW, p.L), BF16)


def both_kernel(
    p, got, bias_one, bias_two, m_in, mid_far, out_far, back_far, last_far, one_far, two_far, back,
    m_mid, m_out, m_back, m_last, slope_one, slope_two, in_sem, out_sem, *scratch,
):
    u_ref, h_ref, g_ref, acc_ref, run_ref, d_ref, e_ref, row_ref, l_ref = scratch
    copies = [
        pltpu.make_async_copy(far, near, in_sem.at[n])
        for n, (far, near) in enumerate(((mid_far, m_mid), (out_far, m_out), (back_far, m_back), (last_far, m_last)))
    ]
    for copy in copies:
        copy.start()
    clear_edges(p, u_ref)
    for zb in range(p.NZB):

        def load(which, f, j, zb=zb):
            value = got[:, f, zb * p.nzb + j, :, :].astype(F32)
            return value[:, which * p.unit : (which + 1) * p.unit]

        def put(f, j, value, zb=zb):
            back[:, f, zb * p.nzb + j, :, :] = value

        def after_in(t, g, value):
            hidden, slope = silu_of_half(value + bias_one[...])
            slope_one[t, pl.ds(p.M * g, p.M), :] = slope.astype(BF16)
            put_window(p, h_ref, g, t, hidden)

        def after_mid(t, g, value):
            _, slope = silu_of_half(value + bias_two[...])
            slope_two[t, pl.ds(p.M * g, p.M), :] = slope.astype(BF16)

        into = first_layer(p, m_in, u_ref, d_ref, after_in)
        middle = middle_layer(p, m_mid, h_ref, e_ref, run_ref, after_mid)
        begin, rest = backward(
            p, functools.partial(load, 1), m_out, m_back, m_last, slope_one, slope_two, put, scratch
        )
        one_copy = pltpu.make_async_copy(slope_one, one_far.at[zb], out_sem.at[0])
        two_copy = pltpu.make_async_copy(slope_two, two_far.at[zb], out_sem.at[1])
        gather_field(p, functools.partial(load, 0), u_ref, row_ref)
        if zb == 0:
            copies[0].wait()
        into.start()
        into.run(middle.start)
        one_copy.start()
        if zb == 0:
            copies[1].wait()
        middle.run(begin)
        two_copy.start()
        if zb == 0:
            copies[2].wait()
            copies[3].wait()
        rest(lambda: None, lambda: None)
        one_copy.wait()
        two_copy.wait()


def back_kernel(
    p, got, before, m_out, back_far, last_far, one_far, two_far, back,
    m_back, m_last, slope_one, slope_two, sem, *scratch,
):
    clear_edges(p, scratch[0])
    for zb in range(p.NZB):
        pairs = [(two_far.at[zb], slope_two), (one_far.at[zb], slope_one)]
        if zb == 0:
            pairs += [(back_far, m_back), (last_far, m_last)]
        copies = [pltpu.make_async_copy(far, near, sem.at[n]) for n, (far, near) in enumerate(pairs)]
        for copy in copies:
            copy.start()

        def load(f, j, zb=zb):
            at = zb * p.nzb + j
            return got[:, f, at, :, :].astype(F32) - before[:, f, at, :, :].astype(F32)

        def put(f, j, value, zb=zb):
            back[:, f, zb * p.nzb + j, :, :] = value

        def others():
            for copy in copies[1:]:
                copy.wait()

        begin, rest = backward(p, load, m_out, m_back, m_last, slope_one, slope_two, put, scratch)
        begin()
        rest(copies[0].wait, others)


def planes(p):
    for t2 in range(p.tl):
        for part in range(2):
            for x2 in range(p.xl):
                yield (t2 * 2 + part) * p.xl + x2, (part, t2, x2)


def pack_kernel(p, equilibrium, cotangent, out, turned, scratch):
    total = 2 * p.unit
    for row, at in planes(p):
        scratch[pl.ds(row, p.nz, stride=total), :] = equilibrium[at].T
        plane = cotangent[at].T
        turned[at] = plane
        scratch[pl.ds(p.unit + row, p.nz, stride=total), :] = plane
    out[...] = scratch[...].reshape(p.nz, total, p.ny).astype(BF16)


def gram_kernel(p, field, got, first, cotangent, gram, scratch):
    scratch[...] = got[...].astype(F32).reshape(p.nz * p.unit, p.ny)
    sums = [jnp.zeros((1, p.ny), F32) for _ in range(3)]
    for row, at in planes(p):
        old = first[at] - cotangent[at]
        new = field[at] - scratch[pl.ds(row, p.nz, stride=p.unit), :] - first[at]
        for n, product in enumerate((old * old, new * old, new * new)):
            sums[n] = sums[n] + jnp.sum(product, axis=0, keepdims=True)
    lane = lax.broadcasted_iota(jnp.int32, (1, 128), 1)
    line = jnp.zeros((1, 128), F32)
    for n in range(3):
        line = jnp.where(lane == n, jnp.sum(sums[n], axis=1, keepdims=True), line)
    gram[...] = jnp.broadcast_to(line[None], gram.shape)


def turn_kernel(p, field, got, first, turned_first, turned_second, scratch):
    scratch[...] = got[...].astype(F32).reshape(p.nz * p.unit, p.ny)
    for row, at in planes(p):
        turned_second[at] = (field[at] - scratch[pl.ds(row, p.nz, stride=p.unit), :]).T
        turned_first[at] = first[at].T


def small_solve(lines, values):
    order = len(values)
    lines = [list(line) for line in lines]
    values = list(values)
    for column in range(order):
        for line in range(column + 1, order):
            factor = lines[line][column] / lines[column][column]
            lines[line] = [a - factor * b for a, b in zip(lines[line], lines[column])]
            values[line] = values[line] - factor * values[column]
    solution = [None] * order
    for line in reversed(range(order)):
        running = values[line]
        for column in range(line + 1, order):
            running = running - lines[line][column] * solution[column]
        solution[line] = running / lines[line][line]
    return solution


def mix_kernel(gathered, first, second, out):
    total = jnp.sum(gathered[...], axis=0)
    g00, g10, g11 = (total[:, n : n + 1] for n in range(3))
    ridge = RIDGE * (g00 + g11) / 2
    one = jnp.ones_like(g00)
    solution = small_solve([[g00 + ridge, g10], [g10, g11 + ridge]], [one, one])
    whole = solution[0] + solution[1]
    alpha = [value / whole for value in solution]
    for part in range(out.shape[0]):
        for t in range(out.shape[1]):
            for x in range(out.shape[2]):
                at = (part, t, x)
                out[at] = alpha[0] * first[at] + alpha[1] * second[at]


def dft_table(length, sign):
    index = np.arange(length)
    angle = 2.0 * math.pi / length * (index[:, None] * index[None, :] % length)
    cosine, sine = np.cos(angle) / math.sqrt(length), sign * np.sin(angle) / math.sqrt(length)
    table = np.block([[cosine, -sine], [sine, cosine]]).astype(np.float32)
    high = table.astype(BF16)
    low = (table - high.astype(np.float32)).astype(BF16)
    return np.concatenate([high, high, low], axis=0)


def transform(value, table):
    high = value.astype(BF16)
    low = (value - high.astype(F32)).astype(BF16)
    return dot(jnp.concatenate([high, low, high], axis=1), table[...])


def turned_images(value, count, rows, columns):
    images = []
    for n in range(count):
        image = value[n * rows : (n + 1) * rows]
        images.append(jnp.concatenate([image[:, :columns].T, image[:, columns:].T], axis=1))
    return jnp.concatenate(images, axis=0)


def normal_sum(real, imag, sens, mask, tables):
    forward_y, forward_z, inverse_z, inverse_y = tables
    coils, nz, ny = sens.shape[1], sens.shape[3], sens.shape[4]
    total_real, total_imag = jnp.zeros((nz, ny), F32), jnp.zeros((nz, ny), F32)
    count = math.gcd(coils, 4)
    groups = [range(first, first + count) for first in range(0, coils, count)]
    values, keeps = [], []
    for group in groups:
        lines, keep = [], []
        for c in group:
            s_real, s_imag = sens[0, c, 0], sens[1, c, 0]
            lines.append(jnp.concatenate([s_real * real - s_imag * imag, s_real * imag + s_imag * real], axis=1))
            line = mask[0, c].astype(F32)
            keep.append(jnp.concatenate([line, line], axis=1))
        values.append(jnp.concatenate(lines, axis=0))
        keeps.append(jnp.concatenate(keep, axis=0))
    values = [transform(value, forward_y) for value in values]
    values = [transform(turned_images(value, count, nz, ny), forward_z) for value in values]
    values = [transform(value * keep, inverse_z) for value, keep in zip(values, keeps)]
    values = [transform(turned_images(value, count, ny, nz), inverse_y) for value in values]
    for group, value in zip(groups, values):
        for n, c in enumerate(group):
            s_real, s_imag = sens[0, c, 0], sens[1, c, 0]
            z_real, z_imag = value[n * nz : (n + 1) * nz, :ny], value[n * nz : (n + 1) * nz, ny:]
            total_real += s_real * z_real + s_imag * z_imag
            total_imag += s_real * z_imag - s_imag * z_real
    return total_real, total_imag


def first_normal_kernel(
    p, cotangent, sens, mask, forward_y, forward_z, inverse_z, inverse_y, point, turned, packed, scratch
):
    x, t = pl.program_id(0), pl.program_id(1)

    @pl.when(t == 0)
    def _():
        for part in range(2):
            for c in range(sens.shape[1]):
                turned[part, c, 0] = sens[part, c, 0].T

    real, imag = cotangent[0, 0, 0], cotangent[1, 0, 0]
    sums = normal_sum(real, imag, turned, mask, (forward_y, forward_z, inverse_z, inverse_y))
    for part, (value, total) in enumerate(zip((real, imag), sums)):
        value = value + value - ETA * total
        point[part, 0, 0] = value
        scratch[pl.ds((t * 2 + part) * p.xl + x, p.nz, stride=p.unit), :] = value

    @pl.when((x == p.xl - 1) & (t == p.tl - 1))
    def _():
        packed[...] = scratch[...].reshape(p.nz, p.unit, p.ny).astype(BF16)


def next_normal_kernel(
    p, point, returned, cotangent, sens, mask, forward_y, forward_z, inverse_z, inverse_y, field, out, scratch
):
    x, t = pl.program_id(0), pl.program_id(1)

    @pl.when((x == 0) & (t == 0))
    def _():
        scratch[...] = returned[...].astype(F32).reshape(p.nz * p.unit, p.ny)

    values = []
    for part in range(2):
        plane = scratch[pl.ds((t * 2 + part) * p.xl + x, p.nz, stride=p.unit), :]
        values.append(point[part, 0, 0] - plane)
        field[part, 0, 0] = values[part]
    sums = normal_sum(values[0], values[1], sens, mask, (forward_y, forward_z, inverse_z, inverse_y))
    for part, (value, total) in enumerate(zip(values, sums)):
        out[part, 0, 0] = cotangent[part, 0, 0] + value - ETA * total


def normal_call(p, kernel, args, specs, outs, out_specs, name, coils, vmem):
    return pl.pallas_call(
        functools.partial(kernel, p),
        grid=(p.xl, p.tl),
        in_specs=specs,
        out_specs=out_specs,
        out_shape=[jax.ShapeDtypeStruct(shape, kind) for shape, kind in outs],
        scratch_shapes=[pltpu.VMEM((p.nz * p.unit, p.ny), F32)],
        compiler_params=pltpu.CompilerParams(vmem_limit_bytes=vmem),
        cost_estimate=pl.CostEstimate(
            flops=p.xl * p.tl * coils * 4 * 3 * 2 * 2 * p.ny * p.nz * 2 * p.nz,
            bytes_accessed=20 << 20,
            transcendentals=0,
        ),
        name=name,
    )(*args)


def call(
    kernel, outs, args, name, scratch=(), flops=1 << 20, moved=4 << 20, vmem=60 << 20, far_args=(), far_outs=()
):
    shapes = [jax.ShapeDtypeStruct(shape, kind) for shape, kind in outs]
    single = len(shapes) == 1
    return pl.pallas_call(
        kernel,
        in_specs=[ANY if n in far_args else VMEM for n in range(len(args))],
        out_specs=VMEM if single else [ANY if n in far_outs else VMEM for n in range(len(shapes))],
        out_shape=shapes[0] if single else shapes,
        scratch_shapes=list(scratch),
        compiler_params=pltpu.CompilerParams(vmem_limit_bytes=vmem),
        cost_estimate=pl.CostEstimate(flops=flops, bytes_accessed=moved, transcendentals=0),
        name=name,
    )(*args)


def flip_kernel(weight):
    return jnp.transpose(jnp.flip(weight, (2, 3, 4)), (1, 0, 2, 3, 4))


def by_offset(weight):
    outs, ins = weight.shape[:2]
    return jnp.transpose(weight, (3, 0, 2, 4, 1)).reshape(3 * outs, 9 * ins)


def exchange(blocks):
    return lax.all_to_all(blocks, AXES, 0, 0, tiled=True)


def per_device(
    equilibrium, cotangent, sensitivity, sampling, weight_in, bias_in, weight_mid, bias_mid, weight_out
):
    _, frames, width, ny, nz = cotangent.shape
    p = Plan(lax.axis_size("readout"), lax.axis_size("frame"), frames, width, ny, nz, weight_in.shape[0])
    coils = sensitivity.shape[1]
    turned_shape = (2, frames, width, nz, ny)
    z_shape = (p.R, p.F, p.zl, p.unit, ny)
    tables = [
        jnp.asarray(dft_table(ny, 1.0)),
        jnp.asarray(dft_table(nz, 1.0)),
        jnp.asarray(dft_table(nz, -1.0)),
        jnp.asarray(dft_table(ny, -1.0)),
    ]
    if ny == nz:
        tables[1], tables[3] = tables[0], tables[2]
    image = pl.BlockSpec((2, 1, 1, nz, ny), lambda x, t: (0, t, x, 0, 0))
    lines = pl.BlockSpec((nz, p.unit, ny), lambda x, t: (0, 0, 0))
    maps = pl.BlockSpec((2, coils, 1, ny, nz), lambda x, t: (0, 0, x, 0, 0))
    turned_maps = pl.BlockSpec((2, coils, 1, nz, ny), lambda x, t: (0, 0, x, 0, 0))
    masks = pl.BlockSpec((1, coils, ny, nz), lambda x, t: (t, 0, 0, 0))
    whole = [pl.BlockSpec(table.shape, lambda x, t: (0, 0)) for table in tables]

    packed, turned = call(
        functools.partial(pack_kernel, p),
        [((nz, 2 * p.unit, ny), BF16), (turned_shape, F32)],
        (equilibrium, cotangent),
        "pack",
        [pltpu.VMEM((nz * 2 * p.unit, ny), F32)],
    )
    got = exchange(packed.reshape(p.D, p.zl, 2 * p.unit, ny)).reshape(p.R, p.F, p.zl, 2 * p.unit, ny)

    picks = [[p.out_rows(g, s) for s in range(p.tl)] for g in range(p.GL)]
    back_in = flip_kernel(weight_in)
    last = jnp.transpose(back_in, (3, 2, 4, 0, 1)).reshape(3, 18, p.ch)
    last = jnp.pad(last, ((0, 0), (0, 6), (0, 0)))
    weight_args = [
        by_offset(weight_in) * jnp.asarray(0.5, BF16),
        jnp.transpose(weight_mid, (2, 3, 4, 0, 1)).reshape(27, p.ch, p.ch),
        by_offset(flip_kernel(weight_out)),
        jnp.transpose(weight_mid, (2, 3, 4, 1, 0)).reshape(27, p.ch, p.ch),
        last,
        bias_in[None, :],
        bias_mid[None, :],
        jnp.asarray(np.stack([p.mid_table(g) for g in p.mid_first()])),
        jnp.asarray(np.stack([np.stack([p.in_table(g, s) for s in range(p.tl)]) for g in range(p.GI)])),
        jnp.asarray(np.stack([np.stack([pick for pick, _ in line]) for line in picks])),
        jnp.asarray(np.stack([np.stack([x[:, None] for _, x in line]) for line in picks])),
        jnp.asarray(np.stack([p.out_cols(g) for g in range(p.GL)])),
    ]
    in_shape = (p.GI, p.tl * WIDE * p.ch, (p.tl + 2) * 3 * p.UW)
    mid_shape = (len(p.mid_first()), 3 * p.M, 3 * p.W)
    last_shape = (p.GL, p.tl, p.part, p.KW)
    bias_shape = (p.M, p.L)
    m_in, m_out, m_mid, m_back, m_last, bias_one, bias_two = call(
        functools.partial(weights_kernel, p),
        [
            (in_shape, BF16), (in_shape, BF16), (mid_shape, BF16), (mid_shape, BF16), (last_shape, BF16),
            (bias_shape, F32), (bias_shape, F32),
        ],
        weight_args,
        "weights",
    )

    point, turned_sens, packed = normal_call(
        p,
        first_normal_kernel,
        [turned, sensitivity, sampling, *tables],
        [image, maps, masks, *whole],
        [(turned_shape, F32), ((2, coils, width, nz, ny), F32), ((nz, p.unit, ny), BF16)],
        [image, turned_maps, lines],
        "normal_one",
        coils,
        60 << 20,
    )
    got_point = exchange(packed.reshape(p.D, p.zl, p.unit, ny)).reshape(z_shape)

    slope = ((p.NZB, p.T, p.rows, p.L), BF16)
    scratch = [
        pltpu.VMEM((p.GI, (p.T + 2) * 3 * p.UW, p.L), BF16),
        pltpu.VMEM((p.G, p.T, 3 * p.W, p.L), BF16),
        pltpu.VMEM((p.T, p.rows, p.L), BF16),
        pltpu.VMEM((p.F + 2, p.R * p.unit, p.L), F32),
        pltpu.VMEM((p.G, 2, p.M, p.L), F32),
        pltpu.VMEM((p.GI, p.tl * WIDE * p.ch, p.L), F32),
        pltpu.VMEM((p.G, 3 * p.M, p.L), F32),
        pltpu.VMEM((p.F, p.nzb, p.R * p.unit, ny), F32),
        pltpu.VMEM((p.GL, p.tl, p.part, p.L), F32),
    ]
    work = 2 * p.NZB * p.T * p.L * p.rows * 9 * p.W
    slope_one, slope_two, back = call(
        functools.partial(both_kernel, p),
        [slope, slope, (z_shape, BF16)],
        [got, bias_one, bias_two, m_in, m_mid, m_out, m_back, m_last],
        "both",
        [
            pltpu.VMEM(mid_shape, BF16),
            pltpu.VMEM(in_shape, BF16),
            pltpu.VMEM(mid_shape, BF16),
            pltpu.VMEM(last_shape, BF16),
            pltpu.VMEM(slope[0][1:], BF16),
            pltpu.VMEM(slope[0][1:], BF16),
            pltpu.SemaphoreType.DMA((4,)),
            pltpu.SemaphoreType.DMA((2,)),
            *scratch,
        ],
        3 * work,
        16 << 20,
        far_args=(4, 5, 6, 7),
        far_outs=(0, 1),
    )
    returned = exchange(back.reshape(p.D, p.zl, p.unit, ny)).reshape(nz, p.unit, ny)
    back_two = call(
        functools.partial(back_kernel, p),
        [(z_shape, BF16)],
        [got_point, back, m_out, m_back, m_last, slope_one, slope_two],
        "back",
        [
            pltpu.VMEM(mid_shape, BF16),
            pltpu.VMEM(last_shape, BF16),
            pltpu.VMEM(slope[0][1:], BF16),
            pltpu.VMEM(slope[0][1:], BF16),
            pltpu.SemaphoreType.DMA((4,)),
            *scratch,
        ],
        3 * work // 2,
        12 << 20,
        far_args=(3, 4, 5, 6),
    )
    returned_two = exchange(back_two.reshape(p.D, p.zl, p.unit, ny)).reshape(nz, p.unit, ny)
    first, point_two = normal_call(
        p,
        next_normal_kernel,
        [point, returned, turned, turned_sens, sampling, *tables],
        [image, lines, image, turned_maps, masks, *whole],
        [(turned_shape, F32), (turned_shape, F32)],
        [image, image],
        "normal_two",
        coils,
        48 << 20,
    )
    lines_scratch = [pltpu.VMEM((nz * p.unit, ny), F32)]
    gram = call(
        functools.partial(gram_kernel, p),
        [((p.D, 1, 128), F32)],
        [point_two, returned_two, first, turned],
        "gram",
        lines_scratch,
        vmem=16 << 20,
    )
    gathered = exchange(gram)
    first_out, second_out = call(
        functools.partial(turn_kernel, p),
        [(cotangent.shape, F32), (cotangent.shape, F32)],
        [point_two, returned_two, first],
        "turn",
        lines_scratch,
        4 << 20,
        16 << 20,
        vmem=16 << 20,
    )
    return call(mix_kernel, [(cotangent.shape, F32)], [gathered, first_out, second_out], "mix", vmem=16 << 20)


def solution(mesh):
    placed = (
        P(None, "frame", "readout", None, None),
        P(None, "frame", "readout", None, None),
        P(None, None, "readout", None, None),
        P("frame", None, None, None),
        P(),
        P(),
        P(),
        P(),
        P(),
    )
    return jax.shard_map(
        per_device,
        mesh=mesh,
        in_specs=placed,
        out_specs=P(None, "frame", "readout", None, None),
        check_vma=False,
    )
```

```python
import functools
import math

import jax
import jax.numpy as jnp
import numpy as np
from jax import lax
from jax.experimental import pallas as pl
from jax.experimental.pallas import tpu as pltpu
from jax.sharding import PartitionSpec as P

ETA = 0.5
RIDGE = 0.0001
AXES = ("readout", "frame")
F32 = jnp.float32
BF16 = jnp.bfloat16
VMEM = pl.BlockSpec(memory_space=pltpu.VMEM)
ANY = pl.BlockSpec(memory_space=pl.ANY)
GROUP = 4
WIDE = 16
LAST = 8


class Plan:
    def __init__(self, devices_x, devices_t, frames, width, ny, nz, channels):
        self.R, self.F, self.tl, self.xl = devices_x, devices_t, frames, width
        self.ny, self.nz, self.ch = ny, nz, channels
        self.D = devices_x * devices_t
        self.T, self.X = frames * devices_t, width * devices_x
        self.zl = nz // self.D
        self.nzb = min(4, self.zl)
        self.NZB = self.zl // self.nzb
        self.L = self.nzb * ny
        self.unit = frames * 2 * width
        self.rows = self.X * channels
        self.M = GROUP * channels
        self.G = self.X // GROUP
        if self.G == 1:
            self.W, self.ws = self.M, [0]
        else:
            self.W = self.M + 32 if self.G == 2 else self.M + 64
            self.ws = [min(max(self.M * g - 32, 0), self.rows - self.W) for g in range(self.G)]
        self.quad = 2 * width
        self.GI = self.X // WIDE
        near = WIDE // width
        extra = 0 if self.GI == 1 else 4
        self.RW = near + extra
        self.UW = self.RW * self.quad
        self.us = [min(max(near * g - extra // 2, 0), devices_x - near - extra) for g in range(self.GI)]
        self.GL = self.X // LAST
        self.near = LAST // width
        wide = LAST * channels
        self.KW = min(wide + (32 if self.GL == 2 else 64), self.rows)
        self.ks = [min(max(wide * g - 32, 0), self.rows - self.KW) for g in range(self.GL)]
        self.part = 6 * self.near * self.unit

    def mid_of(self, g):
        offsets = [self.ws[n] - self.M * n for n in range(self.G)]
        return sorted(set(offsets), reverse=True).index(offsets[g])

    def mid_first(self):
        return [next(g for g in range(self.G) if self.mid_of(g) == n) for n in range(self.mid_of(self.G - 1) + 1)]

    def mid_table(self, g):
        k = np.arange(3 * self.W)
        row = self.ws[g] + k % self.W
        return pack(k // self.W * self.ch + row % self.ch, row // self.ch)

    def in_table(self, g, t2):
        k = np.arange((self.tl + 2) * 3 * self.UW)
        slot, c, rest = k // (3 * self.UW), k // self.UW % 3, k % self.UW
        part, x2, r = rest // (self.xl * self.RW), rest // self.RW % self.xl, self.us[g] + rest % self.RW
        a = slot - t2
        q = np.where((a >= 0) & (a <= 2), (a * 3 + c) * 2 + part, -1)
        return pack(q, r * self.xl + x2)

    def out_rows(self, g, s):
        m = np.arange(2 * 3 * self.near * self.unit)
        target, rest = m // (3 * self.near * self.unit), m % (3 * self.near * self.unit)
        c, rest = rest // (self.near * self.unit), rest % (self.near * self.unit)
        r, rest = self.near * g + rest // self.unit, rest % self.unit
        frame, part, x2 = rest // (2 * self.xl), rest // self.xl % 2, rest % self.xl
        offset = self.tl if s == 0 else -self.tl
        a = s - frame + 1 + np.where(target == 1, offset, 0)
        q = np.where((a >= 0) & (a <= 2), (a * 3 + c) * 2 + part, -1)
        pick = (q[:, None] == np.arange(18)[None, :]).astype(np.float32).astype(BF16)
        return pick, (r * self.xl + x2).astype(np.int32)

    def out_cols(self, g):
        row = self.ks[g] + np.arange(self.KW)
        return pack(row % self.ch, row // self.ch)


def pack(q, position):
    return np.stack([q, position] + [np.zeros_like(q)] * 6).astype(np.int32)


def dot(a, b):
    return jnp.dot(a, b, preferred_element_type=F32)


def one_hot_rows(table, rows, first=0):
    k = table.shape[1]
    index = lax.broadcasted_iota(jnp.int32, (rows, k), 0) + first
    return (index == jnp.broadcast_to(table[0:1, :], (rows, k))).astype(F32).astype(BF16)


def banded(weights, table, first, count, channels, out_ref, where, row0):
    spread = dot(weights, one_hot_rows(table, weights.shape[1]))
    parts = [spread[b * channels : (b + 1) * channels] for b in range(3)]
    position = table[1:2, :]
    for pair in range(count // 2):
        rows = []
        for x in (first + 2 * pair, first + 2 * pair + 1):
            rows.append(
                jnp.where(
                    position == x - 1,
                    parts[0],
                    jnp.where(position == x, parts[1], jnp.where(position == x + 1, parts[2], 0.0)),
                )
            )
        out_ref[where, row0 + 2 * pair * channels : row0 + 2 * (pair + 1) * channels, :] = jnp.concatenate(
            rows, axis=0
        ).astype(BF16)


def tap_stacks(raw, adjoint):
    stacks = []
    for c in range(3):
        blocks = []
        for ab in range(9):
            n = ab * 3 + c
            blocks.append(raw[26 - n].astype(F32).T if adjoint else raw[n].astype(F32))
        stacks.append(jnp.concatenate(blocks, axis=0).astype(BF16))
    return stacks


def pair_stacks(raw, adjoint):
    stacks = []
    for b in range(3):
        taps = [(a * 3 + b) * 3 + c for a in range(3) for c in range(3)]
        rows = [raw[26 - n if adjoint else n].astype(F32) for n in taps]
        stacks.append(jnp.concatenate(rows, axis=0))
    return stacks


def banded_taps(stacks, table, first, channels, out_ref, where, scale):
    spread = None
    for c in range(3):
        part = dot(stacks[c], one_hot_rows(table, channels, c * channels))
        spread = part if spread is None else spread + part
    position = table[1:2, :]
    for a in range(3):
        parts = [spread[(a * 3 + b) * channels : (a * 3 + b + 1) * channels] * scale for b in range(3)]
        for pair in range(GROUP // 2):
            rows = []
            for x in (first + 2 * pair, first + 2 * pair + 1):
                rows.append(
                    jnp.where(
                        position == x - 1,
                        parts[0],
                        jnp.where(position == x, parts[1], jnp.where(position == x + 1, parts[2], 0.0)),
                    )
                )
            at = (a * GROUP + 2 * pair) * channels
            out_ref[where, at : at + 2 * channels, :] = jnp.concatenate(rows, axis=0).astype(BF16)


def weights_kernel(
    p, w_in, w_mid, w_out, one, two, mid_tab, in_tab, pick, row_x, col_tab,
    m_in, m_out, m_mid, m_back, m_last, bias_one, bias_two,
):
    for line, out in ((one, bias_one), (two, bias_two)):
        shape = (p.ch, p.ch)
        same = lax.broadcasted_iota(jnp.int32, shape, 0) == lax.broadcasted_iota(jnp.int32, shape, 1)
        column = 0.5 * jnp.sum(jnp.where(same, line[...], 0.0), axis=1, keepdims=True)
        for n in range(GROUP):
            out[n * p.ch : (n + 1) * p.ch, :] = jnp.broadcast_to(column, (p.ch, p.L))
    forward, adjoint = tap_stacks(w_mid, False), tap_stacks(w_mid, True)
    for n, g in enumerate(p.mid_first()):
        table = mid_tab[n]
        banded_taps(forward, table, g * GROUP, p.ch, m_mid, n, 0.5)
        banded_taps(adjoint, table, g * GROUP, p.ch, m_back, n, 1.0)
    into = (0.5 * jnp.concatenate([stack.T for stack in pair_stacks(w_in, False)], axis=0)).astype(BF16)
    outof = jnp.concatenate([stack.T for stack in pair_stacks(w_out, True)], axis=0).astype(BF16)
    last = [stack.astype(BF16) for stack in pair_stacks(w_in, True)]
    for g in range(p.GI):
        for t2 in range(p.tl):
            table = in_tab[g, t2]
            banded(into, table, g * WIDE, WIDE, p.ch, m_in, g, t2 * WIDE * p.ch)
            banded(outof, table, g * WIDE, WIDE, p.ch, m_out, g, t2 * WIDE * p.ch)
    for g in range(p.GL):
        cols = col_tab[g]
        place = one_hot_rows(cols, p.ch)
        position = cols[1:2, :]
        taps = [dot(last[b], place).astype(BF16) for b in range(3)]
        for s in range(p.tl):
            x = row_x[g, s]
            total = jnp.zeros((x.shape[0], p.KW), F32)
            for b in range(3):
                total = jnp.where(position == x + (b - 1), dot(pick[g, s], taps[b]), total)
            m_last[g, s] = total.astype(BF16)


def shifted(value, c, ny):
    if c == 1:
        return value
    pieces = []
    for at in range(0, value.shape[1], ny):
        piece = value[:, at : at + ny]
        lane = lax.broadcasted_iota(jnp.int32, piece.shape, 1)
        if c == 0:
            pieces.append(jnp.where(lane == 0, jnp.zeros_like(piece), pltpu.roll(piece, 1, 1)))
        else:
            pieces.append(jnp.where(lane == ny - 1, jnp.zeros_like(piece), pltpu.roll(piece, ny - 1, 1)))
    return pieces[0] if len(pieces) == 1 else jnp.concatenate(pieces, axis=1)


def silu_of_half(half):
    double = 1.0 + jnp.tanh(half)
    value = half * double
    sigma = 0.5 * double
    return value, sigma + value * (1.0 - sigma)


def gather_field(p, load, u_ref, row_ref):
    for f in range(p.F):
        for j in range(p.nzb):
            row_ref[f, j] = load(f, j).reshape(p.R * p.unit, p.ny)
        for t2 in range(p.tl):
            lines = []
            for k in range(p.quad):
                start = t2 * p.quad + k
                line = [row_ref[f, j, pl.ds(start, p.R, stride=p.unit), :] for j in range(p.nzb)]
                lines.append(line[0] if p.nzb == 1 else jnp.concatenate(line, axis=1))
            for g in range(p.GI):
                value = jnp.concatenate([line[p.us[g] : p.us[g] + p.RW] for line in lines], axis=0).astype(BF16)
                for c in range(3):
                    start = ((f * p.tl + t2 + 1) * 3 + c) * p.UW
                    u_ref[g, start : start + p.UW, :] = shifted(value, c, p.ny)


def put_window(p, h_ref, g, t, value):
    value = value.astype(BF16)
    for c in range(3):
        moved = shifted(value, c, p.ny)
        for h in range(p.G):
            lo, hi = max(p.M * g, p.ws[h]), min(p.M * (g + 1), p.ws[h] + p.W)
            if lo < hi:
                start = c * p.W + lo - p.ws[h]
                h_ref[h, t, start : start + hi - lo, :] = moved[lo - p.M * g : hi - p.M * g]


class Layer:
    def __init__(self, steps, issue, finish, end=None):
        self.steps, self.issue, self.finish, self.end = steps, issue, finish, end

    def start(self):
        self.issue(0)

    def run(self, ahead=None):
        def body(n, carry):
            self.finish(n - 1)
            self.issue(n)
            return carry

        lax.fori_loop(1, self.steps, body, 0)
        if ahead is not None:
            ahead()
        self.finish(self.steps - 1)
        if self.end is not None:
            self.end()


def first_layer(p, matrix, u_ref, d_ref, each):
    def issue(f):
        start = f * (p.tl * 3 * p.UW)
        if not isinstance(f, int):
            start = pl.multiple_of(start, 16)
        size = (p.tl + 2) * 3 * p.UW
        for gi in range(p.GI):
            d_ref[gi] = dot(matrix[gi], u_ref[gi, pl.ds(start, size), :])

    def finish(f):
        for gi in range(p.GI):
            for t2 in range(p.tl):
                for at in range(WIDE // GROUP):
                    row = (t2 * WIDE + at * GROUP) * p.ch
                    each(f * p.tl + t2, gi * (WIDE // GROUP) + at, d_ref[gi, row : row + p.M, :])

    return Layer(p.F, issue, finish)


def middle_layer(p, matrix, h_ref, d_ref, run_ref, each):
    def issue(t):
        if isinstance(t, int):
            run_ref[...] = jnp.zeros_like(run_ref)
        for g in range(p.G):
            d_ref[g] = dot(matrix[p.mid_of(g)], h_ref[g, t])

    def finish(t):
        for g in range(p.G):
            before = jnp.maximum(t - 1, 0) if not isinstance(t, int) else t - 1
            each(before, g, run_ref[g, 0] + d_ref[g, 2 * p.M :, :])
            run_ref[g, 0] = run_ref[g, 1] + d_ref[g, p.M : 2 * p.M, :]
            run_ref[g, 1] = d_ref[g, : p.M, :]

    def end():
        for g in range(p.G):
            each(p.T - 1, g, run_ref[g, 0])

    return Layer(p.T, issue, finish, end)


def last_layer(p, matrix, g_ref, l_ref, acc_ref):
    size = p.near * p.unit

    def issue(f):
        if isinstance(f, int):
            acc_ref[...] = jnp.zeros_like(acc_ref)
        for g in range(p.GL):
            for s in range(p.tl):
                l_ref[g, s] = dot(matrix[g, s], g_ref[f * p.tl + s, pl.ds(p.ks[g], p.KW), :])

    def finish(f):
        for g in range(p.GL):
            for s in range(p.tl):
                for target in range(2):
                    slot = f + 1 if target == 0 else (f if s == 0 else f + 2)
                    first = target * 3 * size
                    value = l_ref[g, s, first + size : first + 2 * size, :]
                    for c in (0, 2):
                        value = value + shifted(l_ref[g, s, first + c * size : first + (c + 1) * size, :], c, p.ny)
                    acc_ref[slot, pl.ds(g * size, size), :] += value

    return Layer(p.F, issue, finish)


def backward(p, load, m_out, m_back, m_last, slope_one, slope_two, put, scratch):
    u_ref, h_ref, g_ref, acc_ref, run_ref, d_ref, e_ref, row_ref, l_ref = scratch

    def after_out(t, g, value):
        rows = pl.ds(p.M * g, p.M)
        put_window(p, h_ref, g, t, slope_two[t, rows, :].astype(F32) * value)

    def after_mid(t, g, value):
        rows = pl.ds(p.M * g, p.M)
        g_ref[t, rows, :] = (slope_one[t, rows, :].astype(F32) * value).astype(BF16)

    out = first_layer(p, m_out, u_ref, d_ref, after_out)
    middle = middle_layer(p, m_back, h_ref, e_ref, run_ref, after_mid)
    last = last_layer(p, m_last, g_ref, l_ref, acc_ref)

    def begin():
        gather_field(p, load, u_ref, row_ref)
        out.start()

    def rest(before_two, before_one):
        before_two()

        def ahead():
            before_one()
            middle.start()

        out.run(ahead)
        middle.run(last.start)
        last.run()
        for f in range(p.F):
            for j in range(p.nzb):
                value = acc_ref[f + 1, :, j * p.ny : (j + 1) * p.ny].reshape(p.R, p.unit, p.ny)
                put(f, j, value.astype(BF16))

    return begin, rest


def clear_edges(p, u_ref):
    u_ref[:, : 3 * p.UW, :] = jnp.zeros((p.GI, 3 * p.UW, p.L), BF16)
    u_ref[:, (p.T + 1) * 3 * p.UW :, :] = jnp.zeros((p.GI, 3 * p.UW, p.L), BF16)


def both_kernel(
    p, got, bias_one, bias_two, m_in, mid_far, out_far, back_far, last_far, one_far, two_far, back,
    m_mid, m_out, m_back, m_last, slope_one, slope_two, in_sem, out_sem, *scratch,
):
    u_ref, h_ref, g_ref, acc_ref, run_ref, d_ref, e_ref, row_ref, l_ref = scratch
    copies = [
        pltpu.make_async_copy(far, near, in_sem.at[n])
        for n, (far, near) in enumerate(((mid_far, m_mid), (out_far, m_out), (back_far, m_back), (last_far, m_last)))
    ]
    for copy in copies:
        copy.start()
    clear_edges(p, u_ref)
    for zb in range(p.NZB):

        def load(which, f, j, zb=zb):
            value = got[:, f, zb * p.nzb + j, :, :].astype(F32)
            return value[:, which * p.unit : (which + 1) * p.unit]

        def put(f, j, value, zb=zb):
            back[:, f, zb * p.nzb + j, :, :] = value

        def after_in(t, g, value):
            hidden, slope = silu_of_half(value + bias_one[...])
            slope_one[t, pl.ds(p.M * g, p.M), :] = slope.astype(BF16)
            put_window(p, h_ref, g, t, hidden)

        def after_mid(t, g, value):
            _, slope = silu_of_half(value + bias_two[...])
            slope_two[t, pl.ds(p.M * g, p.M), :] = slope.astype(BF16)

        into = first_layer(p, m_in, u_ref, d_ref, after_in)
        middle = middle_layer(p, m_mid, h_ref, e_ref, run_ref, after_mid)
        begin, rest = backward(
            p, functools.partial(load, 1), m_out, m_back, m_last, slope_one, slope_two, put, scratch
        )
        one_copy = pltpu.make_async_copy(slope_one, one_far.at[zb], out_sem.at[0])
        two_copy = pltpu.make_async_copy(slope_two, two_far.at[zb], out_sem.at[1])
        gather_field(p, functools.partial(load, 0), u_ref, row_ref)
        if zb == 0:
            copies[0].wait()
        into.start()
        into.run(middle.start)
        one_copy.start()
        if zb == 0:
            copies[1].wait()
        middle.run(begin)
        two_copy.start()
        if zb == 0:
            copies[2].wait()
            copies[3].wait()
        rest(lambda: None, lambda: None)
        one_copy.wait()
        two_copy.wait()


def back_kernel(
    p, got, before, m_out, back_far, last_far, one_far, two_far, back,
    m_back, m_last, slope_one, slope_two, sem, *scratch,
):
    clear_edges(p, scratch[0])
    for zb in range(p.NZB):
        pairs = [(two_far.at[zb], slope_two), (one_far.at[zb], slope_one)]
        if zb == 0:
            pairs += [(back_far, m_back), (last_far, m_last)]
        copies = [pltpu.make_async_copy(far, near, sem.at[n]) for n, (far, near) in enumerate(pairs)]
        for copy in copies:
            copy.start()

        def load(f, j, zb=zb):
            at = zb * p.nzb + j
            return got[:, f, at, :, :].astype(F32) - before[:, f, at, :, :].astype(F32)

        def put(f, j, value, zb=zb):
            back[:, f, zb * p.nzb + j, :, :] = value

        def others():
            for copy in copies[1:]:
                copy.wait()

        begin, rest = backward(p, load, m_out, m_back, m_last, slope_one, slope_two, put, scratch)
        begin()
        rest(copies[0].wait, others)


def planes(p):
    for t2 in range(p.tl):
        for part in range(2):
            for x2 in range(p.xl):
                yield (t2 * 2 + part) * p.xl + x2, (part, t2, x2)


def pack_kernel(p, equilibrium, cotangent, out, turned, scratch):
    total = 2 * p.unit
    for row, at in planes(p):
        scratch[pl.ds(row, p.nz, stride=total), :] = equilibrium[at].T
        plane = cotangent[at].T
        turned[at] = plane
        scratch[pl.ds(p.unit + row, p.nz, stride=total), :] = plane
    out[...] = scratch[...].reshape(p.nz, total, p.ny).astype(BF16)


def gram_kernel(p, field, got, first, cotangent, gram, scratch):
    scratch[...] = got[...].astype(F32).reshape(p.nz * p.unit, p.ny)
    sums = [jnp.zeros((1, p.ny), F32) for _ in range(3)]
    for row, at in planes(p):
        old = first[at] - cotangent[at]
        new = field[at] - scratch[pl.ds(row, p.nz, stride=p.unit), :] - first[at]
        for n, product in enumerate((old * old, new * old, new * new)):
            sums[n] = sums[n] + jnp.sum(product, axis=0, keepdims=True)
    lane = lax.broadcasted_iota(jnp.int32, (1, 128), 1)
    line = jnp.zeros((1, 128), F32)
    for n in range(3):
        line = jnp.where(lane == n, jnp.sum(sums[n], axis=1, keepdims=True), line)
    gram[...] = jnp.broadcast_to(line[None], gram.shape)


def turn_kernel(p, field, got, first, turned_first, turned_second, scratch):
    scratch[...] = got[...].astype(F32).reshape(p.nz * p.unit, p.ny)
    for row, at in planes(p):
        turned_second[at] = (field[at] - scratch[pl.ds(row, p.nz, stride=p.unit), :]).T
        turned_first[at] = first[at].T


def small_solve(lines, values):
    order = len(values)
    lines = [list(line) for line in lines]
    values = list(values)
    for column in range(order):
        for line in range(column + 1, order):
            factor = lines[line][column] / lines[column][column]
            lines[line] = [a - factor * b for a, b in zip(lines[line], lines[column])]
            values[line] = values[line] - factor * values[column]
    solution = [None] * order
    for line in reversed(range(order)):
        running = values[line]
        for column in range(line + 1, order):
            running = running - lines[line][column] * solution[column]
        solution[line] = running / lines[line][line]
    return solution


def mix_kernel(gathered, first, second, out):
    total = jnp.sum(gathered[...], axis=0)
    g00, g10, g11 = (total[:, n : n + 1] for n in range(3))
    ridge = RIDGE * (g00 + g11) / 2
    one = jnp.ones_like(g00)
    solution = small_solve([[g00 + ridge, g10], [g10, g11 + ridge]], [one, one])
    whole = solution[0] + solution[1]
    alpha = [value / whole for value in solution]
    for part in range(out.shape[0]):
        for t in range(out.shape[1]):
            for x in range(out.shape[2]):
                at = (part, t, x)
                out[at] = alpha[0] * first[at] + alpha[1] * second[at]


def dft_table(length, sign):
    index = np.arange(length)
    angle = 2.0 * math.pi / length * (index[:, None] * index[None, :] % length)
    cosine, sine = np.cos(angle) / math.sqrt(length), sign * np.sin(angle) / math.sqrt(length)
    table = np.block([[cosine, -sine], [sine, cosine]]).astype(np.float32)
    high = table.astype(BF16)
    low = (table - high.astype(np.float32)).astype(BF16)
    return np.concatenate([high, high, low], axis=0)


def transform(value, table):
    high = value.astype(BF16)
    low = (value - high.astype(F32)).astype(BF16)
    return dot(jnp.concatenate([high, low, high], axis=1), table[...])


def turned_images(value, count, rows, columns):
    images = []
    for n in range(count):
        image = value[n * rows : (n + 1) * rows]
        images.append(jnp.concatenate([image[:, :columns].T, image[:, columns:].T], axis=1))
    return jnp.concatenate(images, axis=0)


def normal_sum(real, imag, sens, mask, tables):
    forward_y, forward_z, inverse_z, inverse_y = tables
    coils, nz, ny = sens.shape[1], sens.shape[3], sens.shape[4]
    total_real, total_imag = jnp.zeros((nz, ny), F32), jnp.zeros((nz, ny), F32)
    count = math.gcd(coils, 4)
    groups = [range(first, first + count) for first in range(0, coils, count)]
    values, keeps = [], []
    for group in groups:
        lines, keep = [], []
        for c in group:
            s_real, s_imag = sens[0, c, 0], sens[1, c, 0]
            lines.append(jnp.concatenate([s_real * real - s_imag * imag, s_real * imag + s_imag * real], axis=1))
            line = mask[0, c].astype(F32)
            keep.append(jnp.concatenate([line, line], axis=1))
        values.append(jnp.concatenate(lines, axis=0))
        keeps.append(jnp.concatenate(keep, axis=0))
    values = [transform(value, forward_y) for value in values]
    values = [transform(turned_images(value, count, nz, ny), forward_z) for value in values]
    values = [transform(value * keep, inverse_z) for value, keep in zip(values, keeps)]
    values = [transform(turned_images(value, count, ny, nz), inverse_y) for value in values]
    for group, value in zip(groups, values):
        for n, c in enumerate(group):
            s_real, s_imag = sens[0, c, 0], sens[1, c, 0]
            z_real, z_imag = value[n * nz : (n + 1) * nz, :ny], value[n * nz : (n + 1) * nz, ny:]
            total_real += s_real * z_real + s_imag * z_imag
            total_imag += s_real * z_imag - s_imag * z_real
    return total_real, total_imag


def first_normal_kernel(
    p, cotangent, sens, mask, forward_y, forward_z, inverse_z, inverse_y, point, turned, packed, scratch
):
    x, t = pl.program_id(0), pl.program_id(1)

    @pl.when(t == 0)
    def _():
        for part in range(2):
            for c in range(sens.shape[1]):
                turned[part, c, 0] = sens[part, c, 0].T

    real, imag = cotangent[0, 0, 0], cotangent[1, 0, 0]
    sums = normal_sum(real, imag, turned, mask, (forward_y, forward_z, inverse_z, inverse_y))
    for part, (value, total) in enumerate(zip((real, imag), sums)):
        value = value + value - ETA * total
        point[part, 0, 0] = value
        scratch[pl.ds((t * 2 + part) * p.xl + x, p.nz, stride=p.unit), :] = value

    @pl.when((x == p.xl - 1) & (t == p.tl - 1))
    def _():
        packed[...] = scratch[...].reshape(p.nz, p.unit, p.ny).astype(BF16)


def next_normal_kernel(
    p, point, returned, cotangent, sens, mask, forward_y, forward_z, inverse_z, inverse_y, field, out, scratch
):
    x, t = pl.program_id(0), pl.program_id(1)

    @pl.when((x == 0) & (t == 0))
    def _():
        scratch[...] = returned[...].astype(F32).reshape(p.nz * p.unit, p.ny)

    values = []
    for part in range(2):
        plane = scratch[pl.ds((t * 2 + part) * p.xl + x, p.nz, stride=p.unit), :]
        values.append(point[part, 0, 0] - plane)
        field[part, 0, 0] = values[part]
    sums = normal_sum(values[0], values[1], sens, mask, (forward_y, forward_z, inverse_z, inverse_y))
    for part, (value, total) in enumerate(zip(values, sums)):
        out[part, 0, 0] = cotangent[part, 0, 0] + value - ETA * total


def normal_call(p, kernel, args, specs, outs, out_specs, name, coils, vmem):
    return pl.pallas_call(
        functools.partial(kernel, p),
        grid=(p.xl, p.tl),
        in_specs=specs,
        out_specs=out_specs,
        out_shape=[jax.ShapeDtypeStruct(shape, kind) for shape, kind in outs],
        scratch_shapes=[pltpu.VMEM((p.nz * p.unit, p.ny), F32)],
        compiler_params=pltpu.CompilerParams(vmem_limit_bytes=vmem),
        cost_estimate=pl.CostEstimate(
            flops=p.xl * p.tl * coils * 4 * 3 * 2 * 2 * p.ny * p.nz * 2 * p.nz,
            bytes_accessed=20 << 20,
            transcendentals=0,
        ),
        name=name,
    )(*args)


def call(
    kernel, outs, args, name, scratch=(), flops=1 << 20, moved=4 << 20, vmem=60 << 20, far_args=(), far_outs=()
):
    shapes = [jax.ShapeDtypeStruct(shape, kind) for shape, kind in outs]
    single = len(shapes) == 1
    return pl.pallas_call(
        kernel,
        in_specs=[ANY if n in far_args else VMEM for n in range(len(args))],
        out_specs=VMEM if single else [ANY if n in far_outs else VMEM for n in range(len(shapes))],
        out_shape=shapes[0] if single else shapes,
        scratch_shapes=list(scratch),
        compiler_params=pltpu.CompilerParams(vmem_limit_bytes=vmem),
        cost_estimate=pl.CostEstimate(flops=flops, bytes_accessed=moved, transcendentals=0),
        name=name,
    )(*args)


def exchange(blocks):
    return lax.all_to_all(blocks, AXES, 0, 0, tiled=True)


def per_device(
    equilibrium, cotangent, sensitivity, sampling, weight_in, bias_in, weight_mid, bias_mid, weight_out
):
    _, frames, width, ny, nz = cotangent.shape
    p = Plan(lax.axis_size("readout"), lax.axis_size("frame"), frames, width, ny, nz, weight_in.shape[0])
    coils = sensitivity.shape[1]
    turned_shape = (2, frames, width, nz, ny)
    z_shape = (p.R, p.F, p.zl, p.unit, ny)
    tables = [
        jnp.asarray(dft_table(ny, 1.0)),
        jnp.asarray(dft_table(nz, 1.0)),
        jnp.asarray(dft_table(nz, -1.0)),
        jnp.asarray(dft_table(ny, -1.0)),
    ]
    if ny == nz:
        tables[1], tables[3] = tables[0], tables[2]
    image = pl.BlockSpec((2, 1, 1, nz, ny), lambda x, t: (0, t, x, 0, 0))
    lines = pl.BlockSpec((nz, p.unit, ny), lambda x, t: (0, 0, 0))
    maps = pl.BlockSpec((2, coils, 1, ny, nz), lambda x, t: (0, 0, x, 0, 0))
    turned_maps = pl.BlockSpec((2, coils, 1, nz, ny), lambda x, t: (0, 0, x, 0, 0))
    masks = pl.BlockSpec((1, coils, ny, nz), lambda x, t: (t, 0, 0, 0))
    whole = [pl.BlockSpec(table.shape, lambda x, t: (0, 0)) for table in tables]

    packed, turned = call(
        functools.partial(pack_kernel, p),
        [((nz, 2 * p.unit, ny), BF16), (turned_shape, F32)],
        (equilibrium, cotangent),
        "pack",
        [pltpu.VMEM((nz * 2 * p.unit, ny), F32)],
    )
    got = exchange(packed.reshape(p.D, p.zl, 2 * p.unit, ny)).reshape(p.R, p.F, p.zl, 2 * p.unit, ny)

    picks = [[p.out_rows(g, s) for s in range(p.tl)] for g in range(p.GL)]
    weight_args = [
        jnp.transpose(weight_in, (2, 3, 4, 1, 0)).reshape(27, 2, p.ch),
        jnp.transpose(weight_mid, (2, 3, 4, 0, 1)).reshape(27, p.ch, p.ch),
        jnp.transpose(weight_out, (2, 3, 4, 0, 1)).reshape(27, 2, p.ch),
        bias_in[None, :],
        bias_mid[None, :],
        jnp.asarray(np.stack([p.mid_table(g) for g in p.mid_first()])),
        jnp.asarray(np.stack([np.stack([p.in_table(g, s) for s in range(p.tl)]) for g in range(p.GI)])),
        jnp.asarray(np.stack([np.stack([pick for pick, _ in line]) for line in picks])),
        jnp.asarray(np.stack([np.stack([x[:, None] for _, x in line]) for line in picks])),
        jnp.asarray(np.stack([p.out_cols(g) for g in range(p.GL)])),
    ]
    in_shape = (p.GI, p.tl * WIDE * p.ch, (p.tl + 2) * 3 * p.UW)
    mid_shape = (len(p.mid_first()), 3 * p.M, 3 * p.W)
    last_shape = (p.GL, p.tl, p.part, p.KW)
    bias_shape = (p.M, p.L)
    m_in, m_out, m_mid, m_back, m_last, bias_one, bias_two = call(
        functools.partial(weights_kernel, p),
        [
            (in_shape, BF16), (in_shape, BF16), (mid_shape, BF16), (mid_shape, BF16), (last_shape, BF16),
            (bias_shape, F32), (bias_shape, F32),
        ],
        weight_args,
        "weights",
    )

    point, turned_sens, packed = normal_call(
        p,
        first_normal_kernel,
        [turned, sensitivity, sampling, *tables],
        [image, maps, masks, *whole],
        [(turned_shape, F32), ((2, coils, width, nz, ny), F32), ((nz, p.unit, ny), BF16)],
        [image, turned_maps, lines],
        "normal_one",
        coils,
        60 << 20,
    )
    got_point = exchange(packed.reshape(p.D, p.zl, p.unit, ny)).reshape(z_shape)

    slope = ((p.NZB, p.T, p.rows, p.L), BF16)
    scratch = [
        pltpu.VMEM((p.GI, (p.T + 2) * 3 * p.UW, p.L), BF16),
        pltpu.VMEM((p.G, p.T, 3 * p.W, p.L), BF16),
        pltpu.VMEM((p.T, p.rows, p.L), BF16),
        pltpu.VMEM((p.F + 2, p.R * p.unit, p.L), F32),
        pltpu.VMEM((p.G, 2, p.M, p.L), F32),
        pltpu.VMEM((p.GI, p.tl * WIDE * p.ch, p.L), F32),
        pltpu.VMEM((p.G, 3 * p.M, p.L), F32),
        pltpu.VMEM((p.F, p.nzb, p.R * p.unit, ny), F32),
        pltpu.VMEM((p.GL, p.tl, p.part, p.L), F32),
    ]
    work = 2 * p.NZB * p.T * p.L * p.rows * 9 * p.W
    slope_one, slope_two, back = call(
        functools.partial(both_kernel, p),
        [slope, slope, (z_shape, BF16)],
        [got, bias_one, bias_two, m_in, m_mid, m_out, m_back, m_last],
        "both",
        [
            pltpu.VMEM(mid_shape, BF16),
            pltpu.VMEM(in_shape, BF16),
            pltpu.VMEM(mid_shape, BF16),
            pltpu.VMEM(last_shape, BF16),
            pltpu.VMEM(slope[0][1:], BF16),
            pltpu.VMEM(slope[0][1:], BF16),
            pltpu.SemaphoreType.DMA((4,)),
            pltpu.SemaphoreType.DMA((2,)),
            *scratch,
        ],
        3 * work,
        16 << 20,
        far_args=(4, 5, 6, 7),
        far_outs=(0, 1),
    )
    returned = exchange(back.reshape(p.D, p.zl, p.unit, ny)).reshape(nz, p.unit, ny)
    back_two = call(
        functools.partial(back_kernel, p),
        [(z_shape, BF16)],
        [got_point, back, m_out, m_back, m_last, slope_one, slope_two],
        "back",
        [
            pltpu.VMEM(mid_shape, BF16),
            pltpu.VMEM(last_shape, BF16),
            pltpu.VMEM(slope[0][1:], BF16),
            pltpu.VMEM(slope[0][1:], BF16),
            pltpu.SemaphoreType.DMA((4,)),
            *scratch,
        ],
        3 * work // 2,
        12 << 20,
        far_args=(3, 4, 5, 6),
    )
    returned_two = exchange(back_two.reshape(p.D, p.zl, p.unit, ny)).reshape(nz, p.unit, ny)
    first, point_two = normal_call(
        p,
        next_normal_kernel,
        [point, returned, turned, turned_sens, sampling, *tables],
        [image, lines, image, turned_maps, masks, *whole],
        [(turned_shape, F32), (turned_shape, F32)],
        [image, image],
        "normal_two",
        coils,
        48 << 20,
    )
    lines_scratch = [pltpu.VMEM((nz * p.unit, ny), F32)]
    gram = call(
        functools.partial(gram_kernel, p),
        [((p.D, 1, 128), F32)],
        [point_two, returned_two, first, turned],
        "gram",
        lines_scratch,
        vmem=16 << 20,
    )
    gathered = exchange(gram)
    first_out, second_out = call(
        functools.partial(turn_kernel, p),
        [(cotangent.shape, F32), (cotangent.shape, F32)],
        [point_two, returned_two, first],
        "turn",
        lines_scratch,
        4 << 20,
        16 << 20,
        vmem=16 << 20,
    )
    return call(mix_kernel, [(cotangent.shape, F32)], [gathered, first_out, second_out], "mix", vmem=16 << 20)


def solution(mesh):
    placed = (
        P(None, "frame", "readout", None, None),
        P(None, "frame", "readout", None, None),
        P(None, None, "readout", None, None),
        P("frame", None, None, None),
        P(),
        P(),
        P(),
        P(),
        P(),
    )
    return jax.shard_map(
        per_device,
        mesh=mesh,
        in_specs=placed,
        out_specs=P(None, "frame", "readout", None, None),
        check_vma=False,
    )
```

```python
import functools
import math

import jax
import jax.numpy as jnp
import numpy as np
from jax import lax
from jax.experimental import pallas as pl
from jax.experimental.pallas import tpu as pltpu
from jax.sharding import PartitionSpec as P

ETA = 0.5
RIDGE = 0.0001
AXES = ("readout", "frame")
F32 = jnp.float32
BF16 = jnp.bfloat16
VMEM = pl.BlockSpec(memory_space=pltpu.VMEM)
ANY = pl.BlockSpec(memory_space=pl.ANY)
GROUP = 4
WIDE = 16
LAST = 8


class Plan:
    def __init__(self, devices_x, devices_t, frames, width, ny, nz, channels):
        self.R, self.F, self.tl, self.xl = devices_x, devices_t, frames, width
        self.ny, self.nz, self.ch = ny, nz, channels
        self.D = devices_x * devices_t
        self.T, self.X = frames * devices_t, width * devices_x
        self.zl = nz // self.D
        self.nzb = min(4, self.zl)
        self.NZB = self.zl // self.nzb
        self.L = self.nzb * ny
        self.unit = frames * 2 * width
        self.rows = self.X * channels
        self.M = GROUP * channels
        self.G = self.X // GROUP
        if self.G == 1:
            self.W, self.ws = self.M, [0]
        else:
            self.W = self.M + 32 if self.G == 2 else self.M + 64
            self.ws = [min(max(self.M * g - 32, 0), self.rows - self.W) for g in range(self.G)]
        self.quad = 2 * width
        self.GI = self.X // WIDE
        near = WIDE // width
        extra = 0 if self.GI == 1 else 4
        self.RW = near + extra
        self.UW = self.RW * self.quad
        self.us = [min(max(near * g - extra // 2, 0), devices_x - near - extra) for g in range(self.GI)]
        self.GL = self.X // LAST
        self.near = LAST // width
        wide = LAST * channels
        self.KW = min(wide + (32 if self.GL == 2 else 64), self.rows)
        self.ks = [min(max(wide * g - 32, 0), self.rows - self.KW) for g in range(self.GL)]
        self.part = 6 * self.near * self.unit

    def mid_of(self, g):
        offsets = [self.ws[n] - self.M * n for n in range(self.G)]
        return sorted(set(offsets), reverse=True).index(offsets[g])

    def mid_first(self):
        return [next(g for g in range(self.G) if self.mid_of(g) == n) for n in range(self.mid_of(self.G - 1) + 1)]

    def mid_table(self, g):
        k = np.arange(3 * self.W)
        row = self.ws[g] + k % self.W
        return pack(k // self.W * self.ch + row % self.ch, row // self.ch)

    def in_table(self, g, t2):
        k = np.arange((self.tl + 2) * 3 * self.UW)
        slot, c, rest = k // (3 * self.UW), k // self.UW % 3, k % self.UW
        part, x2, r = rest // (self.xl * self.RW), rest // self.RW % self.xl, self.us[g] + rest % self.RW
        a = slot - t2
        q = np.where((a >= 0) & (a <= 2), (a * 3 + c) * 2 + part, -1)
        return pack(q, r * self.xl + x2)

    def out_rows(self, g, s):
        m = np.arange(2 * 3 * self.near * self.unit)
        target, rest = m // (3 * self.near * self.unit), m % (3 * self.near * self.unit)
        c, rest = rest // (self.near * self.unit), rest % (self.near * self.unit)
        r, rest = self.near * g + rest // self.unit, rest % self.unit
        frame, part, x2 = rest // (2 * self.xl), rest // self.xl % 2, rest % self.xl
        offset = self.tl if s == 0 else -self.tl
        a = s - frame + 1 + np.where(target == 1, offset, 0)
        q = np.where((a >= 0) & (a <= 2), (a * 3 + c) * 2 + part, -1)
        pick = (q[:, None] == np.arange(18)[None, :]).astype(np.float32).astype(BF16)
        return pick, (r * self.xl + x2).astype(np.int32)

    def out_cols(self, g):
        row = self.ks[g] + np.arange(self.KW)
        return pack(row % self.ch, row // self.ch)


def pack(q, position):
    return np.stack([q, position] + [np.zeros_like(q)] * 6).astype(np.int32)


def dot(a, b):
    return jnp.dot(a, b, preferred_element_type=F32)


def one_hot_rows(table, rows, first=0):
    k = table.shape[1]
    index = lax.broadcasted_iota(jnp.int32, (rows, k), 0) + first
    return (index == jnp.broadcast_to(table[0:1, :], (rows, k))).astype(F32).astype(BF16)


def banded(weights, table, first, count, channels, out_ref, where, row0):
    spread = dot(weights, one_hot_rows(table, weights.shape[1]))
    parts = [spread[b * channels : (b + 1) * channels] for b in range(3)]
    position = table[1:2, :]
    for pair in range(count // 2):
        rows = []
        for x in (first + 2 * pair, first + 2 * pair + 1):
            rows.append(
                jnp.where(
                    position == x - 1,
                    parts[0],
                    jnp.where(position == x, parts[1], jnp.where(position == x + 1, parts[2], 0.0)),
                )
            )
        out_ref[where, row0 + 2 * pair * channels : row0 + 2 * (pair + 1) * channels, :] = jnp.concatenate(
            rows, axis=0
        ).astype(BF16)


def tap_stacks(raw, adjoint):
    stacks = []
    for c in range(3):
        blocks = []
        for ab in range(9):
            n = ab * 3 + c
            blocks.append(raw[26 - n].astype(F32).T if adjoint else raw[n].astype(F32))
        stacks.append(jnp.concatenate(blocks, axis=0).astype(BF16))
    return stacks


def pair_stacks(raw, adjoint):
    stacks = []
    for b in range(3):
        taps = [(a * 3 + b) * 3 + c for a in range(3) for c in range(3)]
        rows = [raw[26 - n if adjoint else n].astype(F32) for n in taps]
        stacks.append(jnp.concatenate(rows, axis=0))
    return stacks


def banded_taps(stacks, table, first, channels, out_ref, where, scale):
    spread = None
    for c in range(3):
        part = dot(stacks[c], one_hot_rows(table, channels, c * channels))
        spread = part if spread is None else spread + part
    position = table[1:2, :]
    for a in range(3):
        parts = [spread[(a * 3 + b) * channels : (a * 3 + b + 1) * channels] * scale for b in range(3)]
        for pair in range(GROUP // 2):
            rows = []
            for x in (first + 2 * pair, first + 2 * pair + 1):
                rows.append(
                    jnp.where(
                        position == x - 1,
                        parts[0],
                        jnp.where(position == x, parts[1], jnp.where(position == x + 1, parts[2], 0.0)),
                    )
                )
            at = (a * GROUP + 2 * pair) * channels
            out_ref[where, at : at + 2 * channels, :] = jnp.concatenate(rows, axis=0).astype(BF16)


def weights_kernel(
    p, w_in, w_mid, w_out, one, two, mid_tab, in_tab, pick, row_x, col_tab,
    in_far, out_far, mid_far, back_far, last_far, bias_one, bias_two,
    m_in, m_out, m_mid, m_back, m_last, sem,
):
    for line, out in ((one, bias_one), (two, bias_two)):
        shape = (p.ch, p.ch)
        same = lax.broadcasted_iota(jnp.int32, shape, 0) == lax.broadcasted_iota(jnp.int32, shape, 1)
        column = 0.5 * jnp.sum(jnp.where(same, line[...], 0.0), axis=1, keepdims=True)
        for n in range(GROUP):
            out[n * p.ch : (n + 1) * p.ch, :] = jnp.broadcast_to(column, (p.ch, p.L))
    forward, adjoint = tap_stacks(w_mid, False), tap_stacks(w_mid, True)
    for n, g in enumerate(p.mid_first()):
        table = mid_tab[n]
        banded_taps(forward, table, g * GROUP, p.ch, m_mid, n, 0.5)
        banded_taps(adjoint, table, g * GROUP, p.ch, m_back, n, 1.0)
    pairs = ((m_mid, mid_far), (m_back, back_far), (m_in, in_far), (m_out, out_far), (m_last, last_far))
    copies = [pltpu.make_async_copy(near, far, sem.at[n]) for n, (near, far) in enumerate(pairs)]
    copies[0].start()
    copies[1].start()
    into = (0.5 * jnp.concatenate([stack.T for stack in pair_stacks(w_in, False)], axis=0)).astype(BF16)
    outof = jnp.concatenate([stack.T for stack in pair_stacks(w_out, True)], axis=0).astype(BF16)
    last = [stack.astype(BF16) for stack in pair_stacks(w_in, True)]
    for g in range(p.GI):
        for t2 in range(p.tl):
            table = in_tab[g, t2]
            banded(into, table, g * WIDE, WIDE, p.ch, m_in, g, t2 * WIDE * p.ch)
            banded(outof, table, g * WIDE, WIDE, p.ch, m_out, g, t2 * WIDE * p.ch)
    copies[2].start()
    copies[3].start()
    for g in range(p.GL):
        cols = col_tab[g]
        place = one_hot_rows(cols, p.ch)
        position = cols[1:2, :]
        taps = [dot(last[b], place).astype(BF16) for b in range(3)]
        for s in range(p.tl):
            x = row_x[g, s]
            total = jnp.zeros((x.shape[0], p.KW), F32)
            for b in range(3):
                total = jnp.where(position == x + (b - 1), dot(pick[g, s], taps[b]), total)
            m_last[g, s] = total.astype(BF16)
    copies[4].start()
    for copy in copies:
        copy.wait()


def shifted(value, c, ny):
    if c == 1:
        return value
    pieces = []
    for at in range(0, value.shape[1], ny):
        piece = value[:, at : at + ny]
        lane = lax.broadcasted_iota(jnp.int32, piece.shape, 1)
        if c == 0:
            pieces.append(jnp.where(lane == 0, jnp.zeros_like(piece), pltpu.roll(piece, 1, 1)))
        else:
            pieces.append(jnp.where(lane == ny - 1, jnp.zeros_like(piece), pltpu.roll(piece, ny - 1, 1)))
    return pieces[0] if len(pieces) == 1 else jnp.concatenate(pieces, axis=1)


def silu_of_half(half):
    double = 1.0 + jnp.tanh(half)
    value = half * double
    sigma = 0.5 * double
    return value, sigma + value * (1.0 - sigma)


def gather_field(p, load, u_ref, row_ref):
    for f in range(p.F):
        for j in range(p.nzb):
            row_ref[f, j] = load(f, j).reshape(p.R * p.unit, p.ny)
        for t2 in range(p.tl):
            lines = []
            for k in range(p.quad):
                start = t2 * p.quad + k
                line = [row_ref[f, j, pl.ds(start, p.R, stride=p.unit), :] for j in range(p.nzb)]
                lines.append(line[0] if p.nzb == 1 else jnp.concatenate(line, axis=1))
            for g in range(p.GI):
                value = jnp.concatenate([line[p.us[g] : p.us[g] + p.RW] for line in lines], axis=0).astype(BF16)
                for c in range(3):
                    start = ((f * p.tl + t2 + 1) * 3 + c) * p.UW
                    u_ref[g, start : start + p.UW, :] = shifted(value, c, p.ny)


def put_window(p, h_ref, g, t, value):
    value = value.astype(BF16)
    for c in range(3):
        moved = shifted(value, c, p.ny)
        for h in range(p.G):
            lo, hi = max(p.M * g, p.ws[h]), min(p.M * (g + 1), p.ws[h] + p.W)
            if lo < hi:
                start = c * p.W + lo - p.ws[h]
                h_ref[h, t, start : start + hi - lo, :] = moved[lo - p.M * g : hi - p.M * g]


class Layer:
    def __init__(self, steps, issue, finish, end=None):
        self.steps, self.issue, self.finish, self.end = steps, issue, finish, end

    def start(self):
        self.issue(0)

    def run(self, ahead=None):
        def body(n, carry):
            self.finish(n - 1)
            self.issue(n)
            return carry

        lax.fori_loop(1, self.steps, body, 0)
        if ahead is not None:
            ahead()
        self.finish(self.steps - 1)
        if self.end is not None:
            self.end()


def first_layer(p, matrix, u_ref, d_ref, each):
    def issue(f):
        start = f * (p.tl * 3 * p.UW)
        if not isinstance(f, int):
            start = pl.multiple_of(start, 16)
        size = (p.tl + 2) * 3 * p.UW
        for gi in range(p.GI):
            d_ref[gi] = dot(matrix[gi], u_ref[gi, pl.ds(start, size), :])

    def finish(f):
        for gi in range(p.GI):
            for t2 in range(p.tl):
                for at in range(WIDE // GROUP):
                    row = (t2 * WIDE + at * GROUP) * p.ch
                    each(f * p.tl + t2, gi * (WIDE // GROUP) + at, d_ref[gi, row : row + p.M, :])

    return Layer(p.F, issue, finish)


def middle_layer(p, matrix, h_ref, d_ref, run_ref, each):
    def issue(t):
        if isinstance(t, int):
            run_ref[...] = jnp.zeros_like(run_ref)
        for g in range(p.G):
            d_ref[g] = dot(matrix[p.mid_of(g)], h_ref[g, t])

    def finish(t):
        for g in range(p.G):
            before = jnp.maximum(t - 1, 0) if not isinstance(t, int) else t - 1
            each(before, g, run_ref[g, 0] + d_ref[g, 2 * p.M :, :])
            run_ref[g, 0] = run_ref[g, 1] + d_ref[g, p.M : 2 * p.M, :]
            run_ref[g, 1] = d_ref[g, : p.M, :]

    def end():
        for g in range(p.G):
            each(p.T - 1, g, run_ref[g, 0])

    return Layer(p.T, issue, finish, end)


def last_layer(p, matrix, g_ref, l_ref, acc_ref):
    size = p.near * p.unit

    def issue(f):
        if isinstance(f, int):
            acc_ref[...] = jnp.zeros_like(acc_ref)
        for g in range(p.GL):
            for s in range(p.tl):
                l_ref[g, s] = dot(matrix[g, s], g_ref[f * p.tl + s, pl.ds(p.ks[g], p.KW), :])

    def finish(f):
        for g in range(p.GL):
            for s in range(p.tl):
                for target in range(2):
                    slot = f + 1 if target == 0 else (f if s == 0 else f + 2)
                    first = target * 3 * size
                    value = l_ref[g, s, first + size : first + 2 * size, :]
                    for c in (0, 2):
                        value = value + shifted(l_ref[g, s, first + c * size : first + (c + 1) * size, :], c, p.ny)
                    acc_ref[slot, pl.ds(g * size, size), :] += value

    return Layer(p.F, issue, finish)


def backward(p, load, m_out, m_back, m_last, slope_one, slope_two, put, scratch):
    u_ref, h_ref, g_ref, acc_ref, run_ref, d_ref, e_ref, row_ref, l_ref = scratch

    def after_out(t, g, value):
        rows = pl.ds(p.M * g, p.M)
        put_window(p, h_ref, g, t, slope_two[t, rows, :].astype(F32) * value)

    def after_mid(t, g, value):
        rows = pl.ds(p.M * g, p.M)
        g_ref[t, rows, :] = (slope_one[t, rows, :].astype(F32) * value).astype(BF16)

    out = first_layer(p, m_out, u_ref, d_ref, after_out)
    middle = middle_layer(p, m_back, h_ref, e_ref, run_ref, after_mid)
    last = last_layer(p, m_last, g_ref, l_ref, acc_ref)

    def begin():
        gather_field(p, load, u_ref, row_ref)
        out.start()

    def rest(before_two, before_one):
        before_two()

        def ahead():
            before_one()
            middle.start()

        out.run(ahead)
        middle.run(last.start)
        last.run()
        for f in range(p.F):
            for j in range(p.nzb):
                value = acc_ref[f + 1, :, j * p.ny : (j + 1) * p.ny].reshape(p.R, p.unit, p.ny)
                put(f, j, value.astype(BF16))

    return begin, rest


def clear_edges(p, u_ref):
    u_ref[:, : 3 * p.UW, :] = jnp.zeros((p.GI, 3 * p.UW, p.L), BF16)
    u_ref[:, (p.T + 1) * 3 * p.UW :, :] = jnp.zeros((p.GI, 3 * p.UW, p.L), BF16)


def both_kernel(
    p, got, bias_one, bias_two, m_in, mid_far, out_far, back_far, last_far, one_far, two_far, back,
    m_mid, m_out, m_back, m_last, slope_one, slope_two, in_sem, out_sem, *scratch,
):
    u_ref, h_ref, g_ref, acc_ref, run_ref, d_ref, e_ref, row_ref, l_ref = scratch
    copies = [
        pltpu.make_async_copy(far, near, in_sem.at[n])
        for n, (far, near) in enumerate(((mid_far, m_mid), (out_far, m_out), (back_far, m_back), (last_far, m_last)))
    ]
    for copy in copies:
        copy.start()
    clear_edges(p, u_ref)
    for zb in range(p.NZB):

        def load(which, f, j, zb=zb):
            value = got[:, f, zb * p.nzb + j, :, :].astype(F32)
            return value[:, which * p.unit : (which + 1) * p.unit]

        def put(f, j, value, zb=zb):
            back[:, f, zb * p.nzb + j, :, :] = value

        def after_in(t, g, value):
            hidden, slope = silu_of_half(value + bias_one[...])
            slope_one[t, pl.ds(p.M * g, p.M), :] = slope.astype(BF16)
            put_window(p, h_ref, g, t, hidden)

        def after_mid(t, g, value):
            _, slope = silu_of_half(value + bias_two[...])
            slope_two[t, pl.ds(p.M * g, p.M), :] = slope.astype(BF16)

        into = first_layer(p, m_in, u_ref, d_ref, after_in)
        middle = middle_layer(p, m_mid, h_ref, e_ref, run_ref, after_mid)
        begin, rest = backward(
            p, functools.partial(load, 1), m_out, m_back, m_last, slope_one, slope_two, put, scratch
        )
        one_copy = pltpu.make_async_copy(slope_one, one_far.at[zb], out_sem.at[0])
        two_copy = pltpu.make_async_copy(slope_two, two_far.at[zb], out_sem.at[1])
        gather_field(p, functools.partial(load, 0), u_ref, row_ref)
        if zb == 0:
            copies[0].wait()
        into.start()
        into.run(middle.start)
        one_copy.start()
        if zb == 0:
            copies[1].wait()
        middle.run(begin)
        two_copy.start()
        if zb == 0:
            copies[2].wait()
            copies[3].wait()
        rest(lambda: None, lambda: None)
        one_copy.wait()
        two_copy.wait()


def back_kernel(
    p, got, before, m_out, back_far, last_far, one_far, two_far, back,
    m_back, m_last, slope_one, slope_two, sem, *scratch,
):
    clear_edges(p, scratch[0])
    for zb in range(p.NZB):
        pairs = [(two_far.at[zb], slope_two), (one_far.at[zb], slope_one)]
        if zb == 0:
            pairs += [(back_far, m_back), (last_far, m_last)]
        copies = [pltpu.make_async_copy(far, near, sem.at[n]) for n, (far, near) in enumerate(pairs)]
        for copy in copies:
            copy.start()

        def load(f, j, zb=zb):
            at = zb * p.nzb + j
            return got[:, f, at, :, :].astype(F32) - before[:, f, at, :, :].astype(F32)

        def put(f, j, value, zb=zb):
            back[:, f, zb * p.nzb + j, :, :] = value

        def others():
            for copy in copies[1:]:
                copy.wait()

        begin, rest = backward(p, load, m_out, m_back, m_last, slope_one, slope_two, put, scratch)
        begin()
        rest(copies[0].wait, others)


def planes(p):
    for t2 in range(p.tl):
        for part in range(2):
            for x2 in range(p.xl):
                yield (t2 * 2 + part) * p.xl + x2, (part, t2, x2)


def pack_kernel(p, equilibrium, cotangent, out, turned, scratch):
    total = 2 * p.unit
    for row, at in planes(p):
        scratch[pl.ds(row, p.nz, stride=total), :] = equilibrium[at].T
        plane = cotangent[at].T
        turned[at] = plane
        scratch[pl.ds(p.unit + row, p.nz, stride=total), :] = plane
    out[...] = scratch[...].reshape(p.nz, total, p.ny).astype(BF16)


def gram_kernel(p, field, got, first, cotangent, gram, scratch):
    scratch[...] = got[...].astype(F32).reshape(p.nz * p.unit, p.ny)
    sums = [jnp.zeros((1, p.ny), F32) for _ in range(3)]
    for row, at in planes(p):
        old = first[at] - cotangent[at]
        new = field[at] - scratch[pl.ds(row, p.nz, stride=p.unit), :] - first[at]
        for n, product in enumerate((old * old, new * old, new * new)):
            sums[n] = sums[n] + jnp.sum(product, axis=0, keepdims=True)
    lane = lax.broadcasted_iota(jnp.int32, (1, 128), 1)
    line = jnp.zeros((1, 128), F32)
    for n in range(3):
        line = jnp.where(lane == n, jnp.sum(sums[n], axis=1, keepdims=True), line)
    gram[...] = jnp.broadcast_to(line[None], gram.shape)


def turn_kernel(p, field, got, first, turned_first, turned_second, scratch):
    scratch[...] = got[...].astype(F32).reshape(p.nz * p.unit, p.ny)
    for row, at in planes(p):
        turned_second[at] = (field[at] - scratch[pl.ds(row, p.nz, stride=p.unit), :]).T
        turned_first[at] = first[at].T


def small_solve(lines, values):
    order = len(values)
    lines = [list(line) for line in lines]
    values = list(values)
    for column in range(order):
        for line in range(column + 1, order):
            factor = lines[line][column] / lines[column][column]
            lines[line] = [a - factor * b for a, b in zip(lines[line], lines[column])]
            values[line] = values[line] - factor * values[column]
    solution = [None] * order
    for line in reversed(range(order)):
        running = values[line]
        for column in range(line + 1, order):
            running = running - lines[line][column] * solution[column]
        solution[line] = running / lines[line][line]
    return solution


def mix_kernel(gathered, first, second, out):
    total = jnp.sum(gathered[...], axis=0)
    g00, g10, g11 = (total[:, n : n + 1] for n in range(3))
    ridge = RIDGE * (g00 + g11) / 2
    one = jnp.ones_like(g00)
    solution = small_solve([[g00 + ridge, g10], [g10, g11 + ridge]], [one, one])
    whole = solution[0] + solution[1]
    alpha = [value / whole for value in solution]
    for part in range(out.shape[0]):
        for t in range(out.shape[1]):
            for x in range(out.shape[2]):
                at = (part, t, x)
                out[at] = alpha[0] * first[at] + alpha[1] * second[at]


def dft_table(length, sign):
    index = np.arange(length)
    angle = 2.0 * math.pi / length * (index[:, None] * index[None, :] % length)
    cosine, sine = np.cos(angle) / math.sqrt(length), sign * np.sin(angle) / math.sqrt(length)
    table = np.block([[cosine, -sine], [sine, cosine]]).astype(np.float32)
    high = table.astype(BF16)
    low = (table - high.astype(np.float32)).astype(BF16)
    return np.concatenate([high, high, low], axis=0)


def transform(value, table):
    high = value.astype(BF16)
    low = (value - high.astype(F32)).astype(BF16)
    return dot(jnp.concatenate([high, low, high], axis=1), table[...])


def turned_images(value, count, rows, columns):
    images = []
    for n in range(count):
        image = value[n * rows : (n + 1) * rows]
        images.append(jnp.concatenate([image[:, :columns].T, image[:, columns:].T], axis=1))
    return jnp.concatenate(images, axis=0)


def normal_sum(real, imag, sens, mask, tables):
    forward_y, forward_z, inverse_z, inverse_y = tables
    coils, nz, ny = sens.shape[1], sens.shape[3], sens.shape[4]
    total_real, total_imag = jnp.zeros((nz, ny), F32), jnp.zeros((nz, ny), F32)
    count = math.gcd(coils, 4)
    groups = [range(first, first + count) for first in range(0, coils, count)]
    values, keeps = [], []
    for group in groups:
        lines, keep = [], []
        for c in group:
            s_real, s_imag = sens[0, c, 0], sens[1, c, 0]
            lines.append(jnp.concatenate([s_real * real - s_imag * imag, s_real * imag + s_imag * real], axis=1))
            line = mask[0, c].astype(F32)
            keep.append(jnp.concatenate([line, line], axis=1))
        values.append(jnp.concatenate(lines, axis=0))
        keeps.append(jnp.concatenate(keep, axis=0))
    values = [transform(value, forward_y) for value in values]
    values = [transform(turned_images(value, count, nz, ny), forward_z) for value in values]
    values = [transform(value * keep, inverse_z) for value, keep in zip(values, keeps)]
    values = [transform(turned_images(value, count, ny, nz), inverse_y) for value in values]
    for group, value in zip(groups, values):
        for n, c in enumerate(group):
            s_real, s_imag = sens[0, c, 0], sens[1, c, 0]
            z_real, z_imag = value[n * nz : (n + 1) * nz, :ny], value[n * nz : (n + 1) * nz, ny:]
            total_real += s_real * z_real + s_imag * z_imag
            total_imag += s_real * z_imag - s_imag * z_real
    return total_real, total_imag


def first_normal_kernel(
    p, cotangent, sens, mask, forward_y, forward_z, inverse_z, inverse_y, point, turned, packed, scratch
):
    x, t = pl.program_id(0), pl.program_id(1)

    @pl.when(t == 0)
    def _():
        for part in range(2):
            for c in range(sens.shape[1]):
                turned[part, c, 0] = sens[part, c, 0].T

    real, imag = cotangent[0, 0, 0], cotangent[1, 0, 0]
    sums = normal_sum(real, imag, turned, mask, (forward_y, forward_z, inverse_z, inverse_y))
    for part, (value, total) in enumerate(zip((real, imag), sums)):
        value = value + value - ETA * total
        point[part, 0, 0] = value
        scratch[pl.ds((t * 2 + part) * p.xl + x, p.nz, stride=p.unit), :] = value

    @pl.when((x == p.xl - 1) & (t == p.tl - 1))
    def _():
        packed[...] = scratch[...].reshape(p.nz, p.unit, p.ny).astype(BF16)


def next_normal_kernel(
    p, point, returned, cotangent, sens, mask, forward_y, forward_z, inverse_z, inverse_y, field, out, scratch
):
    x, t = pl.program_id(0), pl.program_id(1)

    @pl.when((x == 0) & (t == 0))
    def _():
        scratch[...] = returned[...].astype(F32).reshape(p.nz * p.unit, p.ny)

    values = []
    for part in range(2):
        plane = scratch[pl.ds((t * 2 + part) * p.xl + x, p.nz, stride=p.unit), :]
        values.append(point[part, 0, 0] - plane)
        field[part, 0, 0] = values[part]
    sums = normal_sum(values[0], values[1], sens, mask, (forward_y, forward_z, inverse_z, inverse_y))
    for part, (value, total) in enumerate(zip(values, sums)):
        out[part, 0, 0] = cotangent[part, 0, 0] + value - ETA * total


def normal_call(p, kernel, args, specs, outs, out_specs, name, coils, vmem):
    return pl.pallas_call(
        functools.partial(kernel, p),
        grid=(p.xl, p.tl),
        in_specs=specs,
        out_specs=out_specs,
        out_shape=[jax.ShapeDtypeStruct(shape, kind) for shape, kind in outs],
        scratch_shapes=[pltpu.VMEM((p.nz * p.unit, p.ny), F32)],
        compiler_params=pltpu.CompilerParams(vmem_limit_bytes=vmem),
        cost_estimate=pl.CostEstimate(
            flops=p.xl * p.tl * coils * 4 * 3 * 2 * 2 * p.ny * p.nz * 2 * p.nz,
            bytes_accessed=20 << 20,
            transcendentals=0,
        ),
        name=name,
    )(*args)


def call(
    kernel, outs, args, name, scratch=(), flops=1 << 20, moved=4 << 20, vmem=60 << 20, far_args=(), far_outs=()
):
    shapes = [jax.ShapeDtypeStruct(shape, kind) for shape, kind in outs]
    single = len(shapes) == 1
    return pl.pallas_call(
        kernel,
        in_specs=[ANY if n in far_args else VMEM for n in range(len(args))],
        out_specs=VMEM if single else [ANY if n in far_outs else VMEM for n in range(len(shapes))],
        out_shape=shapes[0] if single else shapes,
        scratch_shapes=list(scratch),
        compiler_params=pltpu.CompilerParams(vmem_limit_bytes=vmem),
        cost_estimate=pl.CostEstimate(flops=flops, bytes_accessed=moved, transcendentals=0),
        name=name,
    )(*args)


def exchange(blocks):
    return lax.all_to_all(blocks, AXES, 0, 0, tiled=True)


def per_device(
    equilibrium, cotangent, sensitivity, sampling, weight_in, bias_in, weight_mid, bias_mid, weight_out
):
    _, frames, width, ny, nz = cotangent.shape
    p = Plan(lax.axis_size("readout"), lax.axis_size("frame"), frames, width, ny, nz, weight_in.shape[0])
    coils = sensitivity.shape[1]
    turned_shape = (2, frames, width, nz, ny)
    z_shape = (p.R, p.F, p.zl, p.unit, ny)
    tables = [
        jnp.asarray(dft_table(ny, 1.0)),
        jnp.asarray(dft_table(nz, 1.0)),
        jnp.asarray(dft_table(nz, -1.0)),
        jnp.asarray(dft_table(ny, -1.0)),
    ]
    if ny == nz:
        tables[1], tables[3] = tables[0], tables[2]
    image = pl.BlockSpec((2, 1, 1, nz, ny), lambda x, t: (0, t, x, 0, 0))
    lines = pl.BlockSpec((nz, p.unit, ny), lambda x, t: (0, 0, 0))
    maps = pl.BlockSpec((2, coils, 1, ny, nz), lambda x, t: (0, 0, x, 0, 0))
    turned_maps = pl.BlockSpec((2, coils, 1, nz, ny), lambda x, t: (0, 0, x, 0, 0))
    masks = pl.BlockSpec((1, coils, ny, nz), lambda x, t: (t, 0, 0, 0))
    whole = [pl.BlockSpec(table.shape, lambda x, t: (0, 0)) for table in tables]

    packed, turned = call(
        functools.partial(pack_kernel, p),
        [((nz, 2 * p.unit, ny), BF16), (turned_shape, F32)],
        (equilibrium, cotangent),
        "pack",
        [pltpu.VMEM((nz * 2 * p.unit, ny), F32)],
    )
    got = exchange(packed.reshape(p.D, p.zl, 2 * p.unit, ny)).reshape(p.R, p.F, p.zl, 2 * p.unit, ny)

    picks = [[p.out_rows(g, s) for s in range(p.tl)] for g in range(p.GL)]
    weight_args = [
        jnp.transpose(weight_in, (2, 3, 4, 1, 0)).reshape(27, 2, p.ch),
        jnp.transpose(weight_mid, (2, 3, 4, 0, 1)).reshape(27, p.ch, p.ch),
        jnp.transpose(weight_out, (2, 3, 4, 0, 1)).reshape(27, 2, p.ch),
        bias_in[None, :],
        bias_mid[None, :],
        jnp.asarray(np.stack([p.mid_table(g) for g in p.mid_first()])),
        jnp.asarray(np.stack([np.stack([p.in_table(g, s) for s in range(p.tl)]) for g in range(p.GI)])),
        jnp.asarray(np.stack([np.stack([pick for pick, _ in line]) for line in picks])),
        jnp.asarray(np.stack([np.stack([x[:, None] for _, x in line]) for line in picks])),
        jnp.asarray(np.stack([p.out_cols(g) for g in range(p.GL)])),
    ]
    in_shape = (p.GI, p.tl * WIDE * p.ch, (p.tl + 2) * 3 * p.UW)
    mid_shape = (len(p.mid_first()), 3 * p.M, 3 * p.W)
    last_shape = (p.GL, p.tl, p.part, p.KW)
    bias_shape = (p.M, p.L)
    m_in, m_out, m_mid, m_back, m_last, bias_one, bias_two = call(
        functools.partial(weights_kernel, p),
        [
            (in_shape, BF16), (in_shape, BF16), (mid_shape, BF16), (mid_shape, BF16), (last_shape, BF16),
            (bias_shape, F32), (bias_shape, F32),
        ],
        weight_args,
        "weights",
        [pltpu.VMEM(shape, BF16) for shape in (in_shape, in_shape, mid_shape, mid_shape, last_shape)]
        + [pltpu.SemaphoreType.DMA((5,))],
        far_outs=(0, 1, 2, 3, 4),
    )

    point, turned_sens, packed = normal_call(
        p,
        first_normal_kernel,
        [turned, sensitivity, sampling, *tables],
        [image, maps, masks, *whole],
        [(turned_shape, F32), ((2, coils, width, nz, ny), F32), ((nz, p.unit, ny), BF16)],
        [image, turned_maps, lines],
        "normal_one",
        coils,
        60 << 20,
    )
    got_point = exchange(packed.reshape(p.D, p.zl, p.unit, ny)).reshape(z_shape)

    slope = ((p.NZB, p.T, p.rows, p.L), BF16)
    scratch = [
        pltpu.VMEM((p.GI, (p.T + 2) * 3 * p.UW, p.L), BF16),
        pltpu.VMEM((p.G, p.T, 3 * p.W, p.L), BF16),
        pltpu.VMEM((p.T, p.rows, p.L), BF16),
        pltpu.VMEM((p.F + 2, p.R * p.unit, p.L), F32),
        pltpu.VMEM((p.G, 2, p.M, p.L), F32),
        pltpu.VMEM((p.GI, p.tl * WIDE * p.ch, p.L), F32),
        pltpu.VMEM((p.G, 3 * p.M, p.L), F32),
        pltpu.VMEM((p.F, p.nzb, p.R * p.unit, ny), F32),
        pltpu.VMEM((p.GL, p.tl, p.part, p.L), F32),
    ]
    work = 2 * p.NZB * p.T * p.L * p.rows * 9 * p.W
    slope_one, slope_two, back = call(
        functools.partial(both_kernel, p),
        [slope, slope, (z_shape, BF16)],
        [got, bias_one, bias_two, m_in, m_mid, m_out, m_back, m_last],
        "both",
        [
            pltpu.VMEM(mid_shape, BF16),
            pltpu.VMEM(in_shape, BF16),
            pltpu.VMEM(mid_shape, BF16),
            pltpu.VMEM(last_shape, BF16),
            pltpu.VMEM(slope[0][1:], BF16),
            pltpu.VMEM(slope[0][1:], BF16),
            pltpu.SemaphoreType.DMA((4,)),
            pltpu.SemaphoreType.DMA((2,)),
            *scratch,
        ],
        3 * work,
        16 << 20,
        far_args=(4, 5, 6, 7),
        far_outs=(0, 1),
    )
    returned = exchange(back.reshape(p.D, p.zl, p.unit, ny)).reshape(nz, p.unit, ny)
    back_two = call(
        functools.partial(back_kernel, p),
        [(z_shape, BF16)],
        [got_point, back, m_out, m_back, m_last, slope_one, slope_two],
        "back",
        [
            pltpu.VMEM(mid_shape, BF16),
            pltpu.VMEM(last_shape, BF16),
            pltpu.VMEM(slope[0][1:], BF16),
            pltpu.VMEM(slope[0][1:], BF16),
            pltpu.SemaphoreType.DMA((4,)),
            *scratch,
        ],
        3 * work // 2,
        12 << 20,
        far_args=(3, 4, 5, 6),
    )
    returned_two = exchange(back_two.reshape(p.D, p.zl, p.unit, ny)).reshape(nz, p.unit, ny)
    first, point_two = normal_call(
        p,
        next_normal_kernel,
        [point, returned, turned, turned_sens, sampling, *tables],
        [image, lines, image, turned_maps, masks, *whole],
        [(turned_shape, F32), (turned_shape, F32)],
        [image, image],
        "normal_two",
        coils,
        48 << 20,
    )
    lines_scratch = [pltpu.VMEM((nz * p.unit, ny), F32)]
    gram = call(
        functools.partial(gram_kernel, p),
        [((p.D, 1, 128), F32)],
        [point_two, returned_two, first, turned],
        "gram",
        lines_scratch,
        vmem=16 << 20,
    )
    gathered = exchange(gram)
    first_out, second_out = call(
        functools.partial(turn_kernel, p),
        [(cotangent.shape, F32), (cotangent.shape, F32)],
        [point_two, returned_two, first],
        "turn",
        lines_scratch,
        4 << 20,
        16 << 20,
        vmem=16 << 20,
    )
    return call(mix_kernel, [(cotangent.shape, F32)], [gathered, first_out, second_out], "mix", vmem=16 << 20)


def solution(mesh):
    placed = (
        P(None, "frame", "readout", None, None),
        P(None, "frame", "readout", None, None),
        P(None, None, "readout", None, None),
        P("frame", None, None, None),
        P(),
        P(),
        P(),
        P(),
        P(),
    )
    return jax.shard_map(
        per_device,
        mesh=mesh,
        in_specs=placed,
        out_specs=P(None, "frame", "readout", None, None),
        check_vma=False,
    )
```
